512 devices in a mesh: layer: 8 (over y_lo, x), head: 64 (over y_hi, z, core).
Axes of the slice: x: 4, y: 4 (y_hi: 2, y_lo: 2; y = y_hi * 2 + y_lo), z: 16, core: 2. Of those that a mesh axis runs over, the one named last changes fastest.
Arguments:
- queries: bfloat16 [16, 64, 512, 128], P('layer', 'head'), may hold values from -4.5 to 4.5
- keys: bfloat16 [16, 64, 512, 128], P('layer', 'head'), may hold values from -4.5 to 4.5
- head_weight: float32 [16, 40], P('layer'), may hold values from -180 to 180
- slot_head: int32 [64], P('head'), may hold values from 0 to 40, as said below
- target: int32 [512, 512], P('head'), may hold values 0 or 1
Outputs:
- query_grad: bfloat16 [16, 64, 512, 128], P('layer', 'head')
- key_grad: bfloat16 [16, 64, 512, 128], P('layer', 'head')
- weight_grad: float32 [16, 64], P('layer', 'head')
The draws below stay inside these ranges and needn't reach their ends.
Inputs may be any that keep to these rules, and one draw needn't show every extreme that they name: `slot_head`: each head 0 to 39 is held by exactly one slot; every other slot holds 40.
All inputs are finite; a program needn't handle non-finite values. No bound on the sum of `target` on one device may be relied on, other than what follows from the above.
Results may differ from the reference program's by a relative error of at most 0.0051.
Values sent between devices are 32-bit elements; how exact they have to be, the bound alone decides.
A program may use at most 64 MiB of HBM per device.

```python
import jax
import jax.numpy as jnp
from jax import lax

L = 512
HEADS = 40
DH = 128
LAYERS = 16
SLOTS = 64


def pair_draw(key):
    key_q, key_k = jax.random.split(jax.random.fold_in(key, 11), 2)
    shape = (LAYERS, SLOTS, L, DH)
    query = jnp.clip(jax.random.normal(key_q, shape, jnp.float32), -4.5, 4.5)
    keyarr = jnp.clip(jax.random.normal(key_k, shape, jnp.float32), -4.5, 4.5)
    return (query, keyarr)


def draw_queries(key, part):
    return pair_draw(key)[0].astype(jnp.bfloat16)


def draw_keys(key, part):
    return pair_draw(key)[1].astype(jnp.bfloat16)


def draw_slot_head(key, part):
    order = jax.random.permutation(jax.random.fold_in(key, 23), SLOTS)
    return jnp.minimum(order, HEADS).astype(jnp.int32)


def plant(values, stream_key, low, largest):
    dims = values.shape
    place = [jax.random.randint(jax.random.fold_in(stream_key, axis), (), 0, dims[axis]) for axis in range(len(dims))]
    values = values.at[tuple(place)].set(low)
    longest = dims.index(max(dims))
    place[longest] = (place[longest] + 1) % dims[longest]
    return values.at[tuple(place)].set(largest)


def shard_levels(own_key, extent, shards, low, top_value):
    loudness, own = 1.0, jax.random.fold_in(own_key, 6)
    for position, parts in shards:
        heights = jnp.exp(jax.random.uniform(jax.random.fold_in(own, position), (parts,), jnp.float32, low / len(shards), top_value / len(shards)))
        loudness = loudness * jnp.repeat(heights, extent[position] // parts).reshape([-1 if axis == position else 1 for axis in range(len(extent))])
    return loudness


def normal_values(own_key, extent, spread, most, shards=(), held_as=jnp.bfloat16):
    result = jax.random.normal(own_key, extent, jnp.float32) * spread
    if len(shards) > 0:
        result = shard_levels(own_key, extent, shards, -0.22, 0.18) * result
    return jnp.clip(result, min=-most, max=most).astype(held_as)


def setup_inputs(seed: int = 0) -> dict:
    arg_keys = jax.random.split(jax.random.key(seed), 6)
    return {
        "queries": draw_queries(jax.random.fold_in(arg_keys[5], 71), 0),
        "keys": draw_keys(jax.random.fold_in(arg_keys[5], 71), 0),
        "head_weight": normal_values(arg_keys[2], (LAYERS, HEADS), 30.0, 180.0, ((0, 8),), jnp.float32),
        "slot_head": draw_slot_head(jax.random.fold_in(arg_keys[5], 71), 0),
        "target": plant((jax.random.randint(arg_keys[4], (L, L), 0, 16) < 1).astype(jnp.int32), jax.random.fold_in(arg_keys[4], 1), 0, 1),
    }


def pair_maps(query, key):
    scale = DH ** -0.5
    scores = jnp.dot(query, key.T, preferred_element_type=jnp.float32) * scale
    highest = jnp.max(scores, axis=1, keepdims=True)
    expo = jnp.exp(scores - highest)
    probs = expo / jnp.sum(expo, axis=1, keepdims=True)
    sym = probs + probs.T
    rowsum = jnp.sum(sym, axis=1)
    total = jnp.sum(rowsum)
    feature = sym - rowsum[:, None] * rowsum[None, :] / total
    return probs, rowsum, total, feature


def pair_back(query, key, weight, error):
    scale = DH ** -0.5
    probs, rowsum, total, feature = pair_maps(query, key)
    wgrad = jnp.sum(error * feature)
    gmap = weight * error
    u_vec = jnp.sum(gmap * rowsum[None, :], axis=1)
    v_vec = jnp.sum(gmap * rowsum[:, None], axis=0)
    dsym = gmap - (u_vec[:, None] + v_vec[None, :]) / total + jnp.sum(rowsum * u_vec) / (total * total)
    dprobs = dsym + dsym.T
    dscores = probs * (dprobs - jnp.sum(probs * dprobs, axis=1, keepdims=True))
    dscores = dscores.astype(jnp.bfloat16)
    qgrad = (jnp.dot(dscores, key, preferred_element_type=jnp.float32) * scale).astype(jnp.bfloat16)
    kgrad = (jnp.dot(dscores.T, query, preferred_element_type=jnp.float32) * scale).astype(jnp.bfloat16)
    return qgrad, kgrad, wgrad


def reference(queries, keys, head_weight, slot_head, target):
    onehot = (slot_head[:, None] == jnp.arange(HEADS, dtype=jnp.int32)[None, :]).astype(jnp.float32)
    slot_weight = jnp.dot(head_weight, onehot.T, precision=lax.Precision.HIGHEST)
    flat_q = queries.reshape(LAYERS * SLOTS, L, DH)
    flat_k = keys.reshape(LAYERS * SLOTS, L, DH)
    flat_w = slot_weight.reshape(LAYERS * SLOTS)

    def add_pair(total, item):
        query, key, weight = item
        feature = pair_maps(query, key)[3]
        return total + weight * feature, None

    logit, _ = lax.scan(add_pair, jnp.zeros((L, L), jnp.float32), (flat_q, flat_k, flat_w))
    error = jax.nn.sigmoid(logit) - target.astype(jnp.float32)

    def back_pair(item):
        query, key, weight = item
        return pair_back(query, key, weight, error)

    qgrad, kgrad, wgrad = lax.map(back_pair, (flat_q, flat_k, flat_w))
    return (qgrad.reshape(LAYERS, SLOTS, L, DH), kgrad.reshape(LAYERS, SLOTS, L, DH), wgrad.reshape(LAYERS, SLOTS))
```

```python
import jax
import jax.numpy as jnp
from jax import lax
from jax.experimental import pallas as pl
from jax.experimental.pallas import tpu as pltpu
from jax.sharding import PartitionSpec as P

MESH = pl.DeviceIdType.MESH
F32 = jnp.float32
BF16 = jnp.bfloat16
L = 512
DH = 128
TILE = 128
TOTAL = 2.0 * L
OFF = {1: (0, 1), 2: (0, 2), 3: (1, 3), 4: (3, 0), 5: (2, 1), 6: (3, 2)}
DIAG = {0: (0, 1), 7: (3, 2)}
KEEP = (0, 0, 0, 1, 1, 0, 1, 1)
MIRROR = (1, 0, 5, 4, 2, 3, 7, 6)
MIRRORED = (1, 0, 4, 5, 3, 2, 7, 6)
MAIN = 32
ROWS = 40
OFFSETS = sorted(
    ((dx, dy) for dx in range(4) for dy in range(4) if dx or dy),
    key=lambda o: -(min(o[0], 4 - o[0]) + min(o[1], 4 - o[1])),
)


def pick(index, table):
    value = jnp.int32(table[0])
    for k in range(1, len(table)):
        value = jnp.where(index == k, jnp.int32(table[k]), value)
    return value


def slot_weights(slot_ref, hw_ref):
    hw = hw_ref[...]
    lane = lax.broadcasted_iota(jnp.int32, hw.shape, 1)
    return jnp.sum(jnp.where(lane == slot_ref[0], hw, 0.0), axis=1, keepdims=True)


def forward(w, q_ref, k_ref, p_ref, rb_ref, rr_ref, x_ref):
    scale = DH ** (-0.5)
    chunk = 64
    sums = []
    for layer in range(2):

        def body(i, csum, layer=layer):
            rows = pl.ds(pl.multiple_of(i * chunk, chunk), chunk)
            scores = lax.dot_general(
                q_ref[layer, rows, :], k_ref[layer], (((1,), (1,)), ((), ())), preferred_element_type=F32
            )
            highest = jnp.max(scores, axis=1, keepdims=True)
            expo = jnp.exp((scores - highest) * scale)
            probs = expo * (1.0 / jnp.sum(expo, axis=1, keepdims=True))
            p_ref[layer, rows, :] = probs
            return csum + jnp.sum(probs, axis=0, keepdims=True)

        csum = lax.fori_loop(0, L // chunk, body, jnp.zeros((1, L), F32))
        rowsum = 1.0 + csum
        rr_ref[layer : layer + 1, :] = rowsum
        for t in range(4):
            wide = jnp.broadcast_to(rowsum[:, t * TILE : (t + 1) * TILE], (TILE, TILE))
            rb_ref[layer, t * TILE : (t + 1) * TILE, :] = wide.T
        sums.append(rowsum * (w[layer : layer + 1, :] / TOTAL))

    def cut(t):
        return slice(t * TILE, (t + 1) * TILE)

    def half(a, b):
        return w[0:1, :] * p_ref[0, cut(a), cut(b)] + w[1:2, :] * p_ref[1, cut(a), cut(b)]

    def block(a, b):
        outer = rb_ref[0, cut(a), :] * sums[0][:, cut(b)] + rb_ref[1, cut(a), :] * sums[1][:, cut(b)]
        return half(a, b) + half(b, a).T - outer

    row = lax.broadcasted_iota(jnp.int32, (TILE, TILE), 0)
    col = lax.broadcasted_iota(jnp.int32, (TILE, TILE), 1)
    for g in range(8):
        if g in OFF:
            full = block(*OFF[g])
            extra = jnp.zeros((8, TILE), F32)
        else:
            upper = block(DIAG[g][0], DIAG[g][0])
            full = jnp.where(row < col, upper, block(DIAG[g][1], DIAG[g][1]))
            extra = jnp.sum(jnp.where(row == col, upper, 0.0), axis=0, keepdims=True)
            extra = jnp.broadcast_to(extra, (8, TILE))
        for part in range(4):
            x_ref[part % 2, 2 * g + part // 2, 0:MAIN, :] = full[part * MAIN : (part + 1) * MAIN, :]
            x_ref[part % 2, 2 * g + part // 2, MAIN:ROWS, :] = extra


def unpack(o_ref, s_ref):
    row = lax.broadcasted_iota(jnp.int32, (TILE, TILE), 0)
    col = lax.broadcasted_iota(jnp.int32, (TILE, TILE), 1)

    def cut(t):
        return slice(t * TILE, (t + 1) * TILE)

    for g in range(8):
        full = jnp.concatenate([o_ref[part % 2, 2 * g + part // 2, 0:MAIN, :] for part in range(4)], axis=0)
        if g in OFF:
            a, b = OFF[g]
            s_ref[cut(a), cut(b)] = full
            s_ref[cut(b), cut(a)] = full.T
        else:
            a, b = DIAG[g]
            turned = full.T
            diagonal = o_ref[0, 2 * g, MAIN : MAIN + 1, :]
            upper = jnp.where(row < col, full, jnp.where(row == col, diagonal, turned))
            s_ref[cut(a), cut(a)] = upper
            s_ref[cut(b), cut(b)] = jnp.where(row < col, turned, full)


def exchange_kernel(
    slot_ref, hw_ref, target_ref, q_ref, k_ref,
    p_ref, s_ref, rb_ref, rr_ref,
    x_ref, a_ref, y_ref, b_ref, z_ref, za_ref, zb_ref, t_ref, to_ref, ta_ref, tb_ref, tt_ref, piece_ref, o_ref,
    s0, r0, s1, r1, sz, rz, st, rt, s3, r3, s4, r4,
):
    layer_pos = lax.axis_index("layer")
    head_pos = lax.axis_index("head")
    x = layer_pos % 4
    y_lo = layer_pos // 4
    core = head_pos % 2
    z = (head_pos // 2) % 16
    y_hi = head_pos // 32
    y = y_hi * 2 + y_lo
    group = y_hi * 4 + x
    other = 1 - core
    mine = group * 2 + y_lo

    def device(dx=0, dy=0, dz=0, flip=False):
        nx = (x + dx) % 4
        ny = (y + dy) % 4
        nz = (z + dz) % 16
        nc = other if flip else core
        return {"layer": (ny % 2) * 4 + nx, "head": (ny // 2) * 32 + nz * 2 + nc}

    def place(dx, dy):
        nx = (x + dx) % 4
        ny = (y + dy) % 4
        return ((ny // 2) * 4 + nx) * 2 + ny % 2

    def in_group(g, c):
        return {"layer": y_lo * 4 + g % 4, "head": (g // 4) * 32 + z * 2 + c}

    partner = device(flip=True)
    sent_to = pick(group, MIRROR)
    got_from = pick(group, MIRRORED)

    barrier = pltpu.get_barrier_semaphore()
    greeted = [device(dx, dy) for dx, dy in OFFSETS]
    greeted += [device(dz=d) for d in (8, 4, -4, 2, -2, 1, -1)]
    greeted += [partner, in_group(sent_to, other), in_group(got_from, other)]
    for d in greeted:
        pl.semaphore_signal(barrier, inc=1, device_id=d, device_id_type=MESH)

    w = slot_weights(slot_ref, hw_ref)
    forward(w, q_ref, k_ref, p_ref, rb_ref, rr_ref, x_ref)

    pl.semaphore_wait(barrier, len(greeted))

    def copy(src, dst, ssem, rsem, dev):
        return pltpu.make_async_remote_copy(
            src_ref=src, dst_ref=dst, send_sem=ssem, recv_sem=rsem, device_id=dev, device_id_type=MESH
        )

    tile = target_ref.at[:, pl.ds(pl.multiple_of(x * TILE, TILE), TILE)]
    near = [(1, 4), (-1, 6), (-2, 7)]
    far = [(4, 0), (-4, 8), (8, 12)]
    t_near = [copy(tile, t_ref.at[slot], st.at[i], rt.at[i], device(dz=d)) for i, (d, slot) in enumerate(near)]
    for c in t_near:
        c.start()
    t_ref[5] = target_ref[:, pl.ds(pl.multiple_of(x * TILE, TILE), TILE)]

    swaps = []
    for i, (dx, dy) in enumerate(OFFSETS + [(0, 0)]):
        p = place(dx, dy)
        swaps.append(copy(x_ref.at[other, p], a_ref.at[p], s0.at[i], r0.at[i], partner))
        swaps[-1].start()

    plane = []
    for i, (dx, dy) in enumerate(OFFSETS):
        p = place(dx, dy)
        swaps[i].wait_recv()
        y_ref[i] = x_ref[core, p] + a_ref[p]
        plane.append(copy(y_ref.at[i], b_ref.at[i], s1.at[i], r1.at[i], device(dx, dy)))
        plane[-1].start()
    swaps[15].wait_recv()
    total = x_ref[core, mine] + a_ref[mine]

    for c in t_near:
        c.wait_recv()
    t_far = [
        copy(t_ref.at[pl.ds(4, 4)], t_ref.at[pl.ds(slot, 4)], st.at[3 + i], rt.at[3 + i], device(dz=d))
        for i, (d, slot) in enumerate(far)
    ]
    for c in t_far:
        c.start()

    for i in reversed(range(15)):
        plane[i].wait_recv()
        total = total + b_ref[i]
    z_ref[0] = total
    z_near = [
        copy(z_ref.at[0], za_ref.at[i], sz.at[i], rz.at[i], device(dz=d)) for i, d in enumerate((1, -1, -2))
    ]
    for c in z_near:
        c.start()
    for i, c in enumerate(z_near):
        c.wait_recv()
        total = total + za_ref[i]
    z_ref[1] = total
    z_far = [
        copy(z_ref.at[1], zb_ref.at[i], sz.at[3 + i], rz.at[3 + i], device(dz=d)) for i, d in enumerate((4, -4, 8))
    ]
    for c in z_far:
        c.start()

    for c in t_far:
        c.wait_recv()
    for slot in range(16):
        to_ref[(z + slot + 11) % 16] = t_ref[slot]
    keep = pick(group, KEEP)
    kept = to_ref.at[pl.ds(keep * 8, 8)]
    given = to_ref.at[pl.ds((1 - keep) * 8, 8)]
    t_plane = [
        copy(kept, ta_ref.at[core], st.at[6], rt.at[6], partner),
        copy(given, tb_ref.at[core], st.at[7], rt.at[7], in_group(sent_to, core)),
        copy(given, tb_ref.at[core], st.at[8], rt.at[8], in_group(sent_to, other)),
    ]
    for c in t_plane:
        c.start()
    ta_ref[core] = to_ref[pl.ds(keep * 8, 8)]
    copy(kept, ta_ref.at[other], st.at[6], rt.at[6], partner).wait_recv()
    copy(given, tb_ref.at[core], st.at[7], rt.at[7], in_group(sent_to, core)).wait_recv()
    copy(given, tb_ref.at[other], st.at[8], rt.at[8], in_group(sent_to, other)).wait_recv()

    def joined(ref):
        return jnp.concatenate([ref[t % 2, t // 2] for t in range(16)], axis=0).astype(F32)

    row = lax.broadcasted_iota(jnp.int32, (TILE, TILE), 0)
    col = lax.broadcasted_iota(jnp.int32, (TILE, TILE), 1)
    first, second = joined(ta_ref), joined(tb_ref)
    first_t, second_t = first.T, second.T
    folded = jnp.where(row < col, first + first_t, second + second_t)
    on_diagonal = jnp.broadcast_to(group % 7, (TILE, TILE)) == 0
    tt_ref[0:TILE, :] = jnp.where(on_diagonal, folded, first + second_t)
    own = jnp.sum(jnp.where(row == col, first, 0.0), axis=0, keepdims=True)
    targets = tt_ref[pl.ds(pl.multiple_of((y_lo * 2 + core) * MAIN, MAIN), MAIN), :]

    for i, c in enumerate(z_far):
        c.wait_recv()
        total = total + zb_ref[i]
    both = 2.0 * jax.nn.sigmoid(total)
    piece_ref[0:MAIN, :] = both[0:MAIN, :] - targets
    piece_ref[MAIN:ROWS, :] = both[MAIN:ROWS, :] - 2.0 * own

    spread = []
    for i, (dx, dy) in enumerate(OFFSETS):
        spread.append(copy(piece_ref, o_ref.at[core, mine], s3.at[i], r3.at[i], device(dx, dy)))
        spread[-1].start()
    own_out = copy(piece_ref, o_ref.at[core, mine], s4.at[15], r4.at[15], partner)
    own_out.start()
    o_ref[core, mine] = piece_ref[...]

    handed = []
    for i in reversed(range(15)):
        dx, dy = OFFSETS[i]
        p = place(-dx, -dy)
        copy(piece_ref, o_ref.at[core, p], s3.at[i], r3.at[i], device(dx, dy)).wait_recv()
        c = copy(o_ref.at[core, p], o_ref.at[core, p], s4.at[i], r4.at[i], partner)
        c.start()
        handed.append(c)
    for i in list(reversed(range(15))):
        dx, dy = OFFSETS[i]
        p = place(-dx, -dy)
        copy(o_ref.at[core, p], o_ref.at[other, p], s4.at[i], r4.at[i], partner).wait_recv()
    copy(piece_ref, o_ref.at[other, mine], s4.at[15], r4.at[15], partner).wait_recv()

    unpack(o_ref, s_ref)

    for c in t_near + t_far + t_plane + swaps + plane + z_near + z_far + spread + handed + [own_out]:
        c.wait_send()


def back_kernel(slot_ref, hw_ref, q_ref, k_ref, p_ref, s_ref, rb_ref, rr_ref, qg_ref, kg_ref, wg_ref, sb_ref, ds_ref):
    scale = DH ** (-0.5)
    w = slot_weights(slot_ref, hw_ref)
    chunk = 32
    zero = jnp.zeros((8, L), F32)

    def rows_of(i):
        return pl.ds(pl.multiple_of(i * chunk, chunk), chunk)

    def gather(i, carry):
        s = s_ref[rows_of(i), :]
        sb_ref[rows_of(i), :] = s.astype(BF16)
        out = []
        for layer in range(2):
            wide = jnp.concatenate([rb_ref[layer, rows_of(i), :]] * 4, axis=1)
            prod = s * wide
            acc = carry[layer]
            for t in range(chunk // 8):
                acc = acc + prod[t * 8 : (t + 1) * 8, :]
            out.append(acc)
        return tuple(out)

    sums = lax.fori_loop(0, L // chunk, gather, (zero, zero))
    for layer in range(2):
        h_row = jnp.sum(sums[layer], axis=0, keepdims=True)
        quad = jnp.sum(h_row * rr_ref[layer : layer + 1, :], axis=1, keepdims=True)
        h_col = jnp.dot(sb_ref[...], rb_ref[layer].astype(BF16), preferred_element_type=F32)
        ds_col = quad * (1.0 / (TOTAL * TOTAL)) - h_col * (1.0 / TOTAL)
        h_scaled = h_row * (1.0 / TOTAL)
        acc = zero
        for i in range(L // chunk):
            rows = slice(i * chunk, (i + 1) * chunk)
            s = s_ref[rows, :]
            probs = p_ref[layer, rows, :]
            wide = jnp.concatenate([ds_col[rows, :]] * 4, axis=1)
            dprobs = s + wide - h_scaled
            prod = probs * s
            for t in range(chunk // 8):
                acc = acc + prod[t * 8 : (t + 1) * 8, :]
            inner = jnp.sum(probs * dprobs, axis=1, keepdims=True)
            ds_ref[rows, :] = (probs * (dprobs - inner)).astype(BF16)
        wg_ref[layer : layer + 1, :] = jnp.sum(
            jnp.sum(acc, axis=0, keepdims=True), axis=1, keepdims=True
        ) - quad * (0.5 / TOTAL)
        factor = w[layer : layer + 1, :] * scale
        qg = jnp.dot(ds_ref[...], k_ref[layer], preferred_element_type=F32)
        qg_ref[layer] = (qg * factor).astype(BF16)
        kg = lax.dot_general(
            ds_ref[...], q_ref[layer], (((0,), (0,)), ((), ())), preferred_element_type=F32
        )
        kg_ref[layer] = (kg * factor).astype(BF16)


def vmem():
    return pl.BlockSpec(memory_space=pltpu.VMEM)


def smem():
    return pl.BlockSpec(memory_space=pltpu.SMEM)


def on_device(queries, keys, head_weight, slot_head, target):
    q = queries.reshape(2, L, DH)
    k = keys.reshape(2, L, DH)
    dma = pltpu.SemaphoreType.DMA
    probs, s_map, rb, rr = pl.pallas_call(
        exchange_kernel,
        out_shape=(
            jax.ShapeDtypeStruct((2, L, L), F32),
            jax.ShapeDtypeStruct((L, L), F32),
            jax.ShapeDtypeStruct((2, L, TILE), F32),
            jax.ShapeDtypeStruct((2, L), F32),
        ),
        in_specs=[smem(), vmem(), vmem(), vmem(), vmem()],
        out_specs=(vmem(), vmem(), vmem(), vmem()),
        scratch_shapes=[
            pltpu.VMEM((2, 16, ROWS, TILE), F32),
            pltpu.VMEM((16, ROWS, TILE), F32),
            pltpu.VMEM((15, ROWS, TILE), F32),
            pltpu.VMEM((15, ROWS, TILE), F32),
            pltpu.VMEM((2, ROWS, TILE), F32),
            pltpu.VMEM((3, ROWS, TILE), F32),
            pltpu.VMEM((3, ROWS, TILE), F32),
            pltpu.VMEM((16, 8, TILE), jnp.int32),
            pltpu.VMEM((16, 8, TILE), jnp.int32),
            pltpu.VMEM((2, 8, 8, TILE), jnp.int32),
            pltpu.VMEM((2, 8, 8, TILE), jnp.int32),
            pltpu.VMEM((TILE, TILE), F32),
            pltpu.VMEM((ROWS, TILE), F32),
            pltpu.VMEM((2, 16, ROWS, TILE), F32),
            dma((16,)), dma((16,)), dma((15,)), dma((15,)), dma((6,)), dma((6,)),
            dma((9,)), dma((9,)), dma((15,)), dma((15,)), dma((16,)), dma((16,)),
        ],
        compiler_params=pltpu.CompilerParams(collective_id=0, has_side_effects=True),
    )(slot_head, head_weight, target, q, k)
    qg, kg, wg = pl.pallas_call(
        back_kernel,
        out_shape=(
            jax.ShapeDtypeStruct((2, L, DH), BF16),
            jax.ShapeDtypeStruct((2, L, DH), BF16),
            jax.ShapeDtypeStruct((2, 1), F32),
        ),
        in_specs=[smem()] + [vmem()] * 7,
        out_specs=(vmem(), vmem(), vmem()),
        scratch_shapes=[pltpu.VMEM((L, L), BF16), pltpu.VMEM((L, L), BF16)],
    )(slot_head, head_weight, q, k, probs, s_map, rb, rr)
    return (qg.reshape(2, 1, L, DH), kg.reshape(2, 1, L, DH), wg)


def solution(mesh):
    placed = (
        P("layer", "head", None, None),
        P("layer", "head", None, None),
        P("layer", None),
        P("head"),
        P("head", None),
    )
    return jax.shard_map(
        on_device,
        mesh=mesh,
        in_specs=placed,
        out_specs=(P("layer", "head", None, None), P("layer", "head", None, None), P("layer", "head")),
        check_vma=False,
    )
```

```python
import jax
import jax.numpy as jnp
from jax import lax
from jax.experimental import pallas as pl
from jax.experimental.pallas import tpu as pltpu
from jax.sharding import PartitionSpec as P

MESH = pl.DeviceIdType.MESH
F32 = jnp.float32
BF16 = jnp.bfloat16
L = 512
DH = 128
TILE = 128
TOTAL = 2.0 * L
OFF = {1: (0, 1), 2: (0, 2), 3: (1, 3), 4: (3, 0), 5: (2, 1), 6: (3, 2)}
DIAG = {0: (0, 1), 7: (3, 2)}
KEEP = (0, 0, 0, 1, 1, 0, 1, 1)
MIRROR = (1, 0, 5, 4, 2, 3, 7, 6)
MIRRORED = (1, 0, 4, 5, 3, 2, 7, 6)
ROWS = 32
OFFSETS = sorted(
    ((dx, dy) for dx in range(4) for dy in range(4) if dx or dy),
    key=lambda o: -(min(o[0], 4 - o[0]) + min(o[1], 4 - o[1])),
)


def pick(index, table):
    value = jnp.int32(table[0])
    for k in range(1, len(table)):
        value = jnp.where(index == k, jnp.int32(table[k]), value)
    return value


def slot_weights(slot_ref, hw_ref):
    hw = hw_ref[...]
    lane = lax.broadcasted_iota(jnp.int32, hw.shape, 1)
    return jnp.sum(jnp.where(lane == slot_ref[0], hw, 0.0), axis=1, keepdims=True)


def forward(w, qk_ref, ready, sc_ref, p_ref, rb_ref, rr_ref, x_ref, e_ref):
    scale = DH ** (-0.5)
    chunk = 32
    sums = []
    for layer in range(2):
        ready(layer)
        sc_ref[...] = lax.dot_general(
            qk_ref[layer, 0], qk_ref[layer, 1], (((1,), (1,)), ((), ())), preferred_element_type=F32
        )

        def body(i, csum, layer=layer):
            rows = pl.ds(pl.multiple_of(i * chunk, chunk), chunk)
            scores = sc_ref[rows, :]
            highest = jnp.max(scores, axis=1, keepdims=True)
            expo = jnp.exp((scores - highest) * scale)
            probs = expo * (1.0 / jnp.sum(expo, axis=1, keepdims=True))
            p_ref[layer, rows, :] = probs
            for t in range(chunk // 8):
                csum = csum + probs[t * 8 : (t + 1) * 8, :]
            return csum

        csum = lax.fori_loop(0, L // chunk, body, jnp.zeros((8, L), F32), unroll=4)
        rowsum = 1.0 + jnp.sum(csum, axis=0, keepdims=True)
        rr_ref[layer : layer + 1, :] = rowsum
        for t in range(4):
            wide = jnp.broadcast_to(rowsum[:, t * TILE : (t + 1) * TILE], (TILE, TILE))
            rb_ref[layer, t * TILE : (t + 1) * TILE, :] = wide.T
        sums.append(rowsum * (w[layer : layer + 1, 0:1] / TOTAL))

    def cut(t):
        return slice(t * TILE, (t + 1) * TILE)

    def half(a, b):
        return w[0:1, :] * p_ref[0, cut(a), cut(b)] + w[1:2, :] * p_ref[1, cut(a), cut(b)]

    def block(a, b):
        outer = rb_ref[0, cut(a), :] * sums[0][:, cut(b)] + rb_ref[1, cut(a), :] * sums[1][:, cut(b)]
        return half(a, b) + half(b, a).T - outer

    row = lax.broadcasted_iota(jnp.int32, (TILE, TILE), 0)
    col = lax.broadcasted_iota(jnp.int32, (TILE, TILE), 1)
    for g in range(8):
        if g in OFF:
            full = block(*OFF[g])
        else:
            upper = block(DIAG[g][0], DIAG[g][0])
            full = jnp.where(row < col, upper, block(DIAG[g][1], DIAG[g][1]))
            extra = jnp.sum(jnp.where(row == col, upper, 0.0), axis=0, keepdims=True)
            e_ref[g // 7] = jnp.broadcast_to(extra, (8, TILE))
        for part in range(4):
            x_ref[part % 2, 2 * g + part // 2] = full[part * ROWS : (part + 1) * ROWS, :]


def unpack(o_ref, eo_ref, s_ref):
    row = lax.broadcasted_iota(jnp.int32, (TILE, TILE), 0)
    col = lax.broadcasted_iota(jnp.int32, (TILE, TILE), 1)

    def cut(t):
        return slice(t * TILE, (t + 1) * TILE)

    for g in range(8):
        full = jnp.concatenate([o_ref[part % 2, 2 * g + part // 2] for part in range(4)], axis=0)
        if g in OFF:
            a, b = OFF[g]
            s_ref[cut(a), cut(b)] = full
            s_ref[cut(b), cut(a)] = full.T
        else:
            a, b = DIAG[g]
            turned = full.T
            diagonal = eo_ref[g // 7, 0:1, :]
            upper = jnp.where(row < col, full, jnp.where(row == col, diagonal, turned))
            s_ref[cut(a), cut(a)] = upper
            s_ref[cut(b), cut(b)] = jnp.where(row < col, turned, full)


def exchange_kernel(
    slot_ref, hw_hbm, target_hbm, q_hbm, k_hbm,
    p_ref, s_ref, rb_ref, rr_ref, w_ref, qk_ref, qt_ref,
    hw_ref, target_ref, sc_ref, x_ref, a_ref, y_ref, b_ref, z_ref, zn_ref, zf_ref,
    t_ref, to_ref, ta_ref, tb_ref, tt_ref, piece_ref, o_ref,
    e_ref, ey_ref, eb_ref, ez_ref, en_ref, ef_ref, ep_ref, eo_ref,
    sin, s0, r0, s1, r1, sz, rz, st, rt, s3, r3, s4, r4, es, er,
):
    loads = [
        pltpu.make_async_copy(q_hbm.at[0], qk_ref.at[0, 0], sin.at[0]),
        pltpu.make_async_copy(k_hbm.at[0], qk_ref.at[0, 1], sin.at[0]),
        pltpu.make_async_copy(hw_hbm, hw_ref, sin.at[2]),
        pltpu.make_async_copy(q_hbm.at[1], qk_ref.at[1, 0], sin.at[1]),
        pltpu.make_async_copy(k_hbm.at[1], qk_ref.at[1, 1], sin.at[1]),
        pltpu.make_async_copy(target_hbm, target_ref, sin.at[3]),
    ]
    for c in loads:
        c.start()
    layer_pos = lax.axis_index("layer")
    head_pos = lax.axis_index("head")
    x = layer_pos % 4
    y_lo = layer_pos // 4
    core = head_pos % 2
    z = (head_pos // 2) % 16
    y_hi = head_pos // 32
    y = y_hi * 2 + y_lo
    group = y_hi * 4 + x
    other = 1 - core
    mine = group * 2 + y_lo

    def device(dx=0, dy=0, dz=0, flip=False):
        nx = (x + dx) % 4
        ny = (y + dy) % 4
        nz = (z + dz) % 16
        nc = other if flip else core
        return {"layer": (ny % 2) * 4 + nx, "head": (ny // 2) * 32 + nz * 2 + nc}

    def place(dx, dy):
        nx = (x + dx) % 4
        ny = (y + dy) % 4
        return ((ny // 2) * 4 + nx) * 2 + ny % 2

    def in_group(g, c):
        return {"layer": y_lo * 4 + g % 4, "head": (g // 4) * 32 + z * 2 + c}

    partner = device(flip=True)
    sent_to = pick(group, MIRROR)
    got_from = pick(group, MIRRORED)

    barrier = pltpu.get_barrier_semaphore()
    greeted = [device(dz=d) for d in (8, 5, -5, 2, -2, 1, -1)]
    greeted += [device(dx, dy) for dx, dy in OFFSETS]
    greeted += [partner, in_group(sent_to, other), in_group(got_from, other)]
    for d in greeted:
        pl.semaphore_signal(barrier, inc=1, device_id=d, device_id_type=MESH)

    def ready(layer):
        pltpu.make_async_copy(qk_ref.at[layer], qk_ref.at[layer], sin.at[layer]).wait()
        if layer == 0:
            loads[2].wait()
            w = slot_weights(slot_ref, hw_ref)
            w_ref[...] = jnp.broadcast_to(w, (2, TILE))

    forward(w_ref, qk_ref, ready, sc_ref, p_ref, rb_ref, rr_ref, x_ref, e_ref)
    loads[5].wait()
    pl.semaphore_wait(barrier, len(greeted))

    def copy(src, dst, ssem, rsem, dev):
        return pltpu.make_async_remote_copy(
            src_ref=src, dst_ref=dst, send_sem=ssem, recv_sem=rsem, device_id=dev, device_id_type=MESH
        )

    def arrived(ref, rsem):
        copy(ref, ref, s0, rsem, partner).wait_recv()

    def left(ref, ssem):
        copy(ref, ref, ssem, r1, partner).wait_send()

    tile = target_ref.at[:, pl.ds(pl.multiple_of(x * TILE, TILE), TILE)]
    for d, slot in ((1, 6), (-1, 8), (2, 5), (-2, 9)):
        copy(tile, t_ref.at[slot], st.at[0], rt.at[0], device(dz=d)).start()
    copy(tile, t_ref.at[15], st.at[0], rt.at[1], device(dz=8)).start()
    t_ref[7] = target_ref[:, pl.ds(pl.multiple_of(x * TILE, TILE), TILE)]

    order = OFFSETS + [(0, 0)]
    for i, (dx, dy) in enumerate(order):
        copy(x_ref.at[other, place(dx, dy)], a_ref.at[pl.ds(i * ROWS, ROWS)], s0, r0.at[i // 4], partner).start()
    copy(e_ref.at[other], a_ref.at[pl.ds(16 * ROWS, 8)], s0, r0.at[3], partner).start()

    for i, (dx, dy) in enumerate(order):
        if i % 4 == 0:
            arrived(a_ref.at[pl.ds(i * ROWS, 4 * ROWS + (8 if i == 12 else 0))], r0.at[i // 4])
        summed = x_ref[core, place(dx, dy)] + a_ref[i * ROWS : (i + 1) * ROWS, :]
        if i < 15:
            y_ref[i] = summed
            copy(y_ref.at[i], b_ref.at[i], s1, r1, device(dx, dy)).start()
        else:
            total = summed

    ey_ref[...] = e_ref[core] + a_ref[16 * ROWS : 16 * ROWS + 8, :]
    owner = mine == core * 14
    owner_of_diagonal = {"layer": core * 3, "head": core * 33 + z * 2}

    @pl.when(jnp.logical_not(owner))
    def _():
        copy(ey_ref, eb_ref.at[mine], es.at[0], er.at[0], owner_of_diagonal).start()

    arrived(t_ref.at[pl.ds(5, 4)], rt.at[0])
    copy(t_ref.at[pl.ds(5, 5)], t_ref.at[pl.ds(0, 5)], st.at[0], rt.at[1], device(dz=5)).start()
    copy(t_ref.at[pl.ds(5, 5)], t_ref.at[pl.ds(10, 5)], st.at[0], rt.at[1], device(dz=-5)).start()

    arrived(b_ref, r1)
    for i in range(15):
        total = total + b_ref[i]
    z_ref[0] = total
    near = (1, -1, 2, -2)
    for i, d in enumerate(near):
        copy(z_ref.at[0], zn_ref.at[i], sz.at[0], rz.at[0], device(dz=d)).start()
    copy(z_ref.at[0], zn_ref.at[4], sz.at[0], rz.at[2], device(dz=8)).start()

    @pl.when(owner)
    def _():
        eb_ref[mine] = ey_ref[...]
        arrived(eb_ref.at[pl.ds(0, 15)], er.at[0])
        acc = eb_ref[0]
        for i in range(1, 16):
            acc = acc + eb_ref[i]
        ez_ref[0] = acc
        for i, d in enumerate(near):
            copy(ez_ref.at[0], en_ref.at[i], es.at[1], er.at[1], device(dz=d)).start()
        copy(ez_ref.at[0], en_ref.at[4], es.at[1], er.at[3], device(dz=8)).start()

    arrived(t_ref.at[pl.ds(0, 11)], rt.at[1])
    for slot in range(16):
        to_ref[(z + slot + 9) % 16] = t_ref[slot]
    keep = pick(group, KEEP)
    kept = to_ref.at[pl.ds(keep * 8, 8)]
    given = to_ref.at[pl.ds((1 - keep) * 8, 8)]
    copy(kept, ta_ref.at[core], st.at[1], rt.at[2], partner).start()
    copy(given, tb_ref.at[core], st.at[2], rt.at[3], in_group(sent_to, core)).start()
    copy(given, tb_ref.at[core], st.at[2], rt.at[3], in_group(sent_to, other)).start()
    ta_ref[core] = to_ref[pl.ds(keep * 8, 8)]
    arrived(zn_ref.at[pl.ds(0, 4)], rz.at[0])
    for i in range(4):
        total = total + zn_ref[i]
    z_ref[1] = total
    for i, d in enumerate((5, -5)):
        copy(z_ref.at[1], zf_ref.at[i], sz.at[1], rz.at[1], device(dz=d)).start()

    @pl.when(owner)
    def _():
        arrived(en_ref.at[pl.ds(0, 4)], er.at[1])
        acc = ez_ref[0]
        for i in range(4):
            acc = acc + en_ref[i]
        ez_ref[1] = acc
        for i, d in enumerate((5, -5)):
            copy(ez_ref.at[1], ef_ref.at[i], es.at[2], er.at[2], device(dz=d)).start()

    for layer in range(2):
        qt_ref[layer] = qk_ref[layer, 0].astype(F32).T.astype(BF16)

    arrived(ta_ref.at[other], rt.at[2])
    arrived(tb_ref, rt.at[3])

    def joined(ref):
        return jnp.concatenate([ref[t % 2, t // 2] for t in range(16)], axis=0).astype(F32)

    row = lax.broadcasted_iota(jnp.int32, (TILE, TILE), 0)
    col = lax.broadcasted_iota(jnp.int32, (TILE, TILE), 1)
    first, second = joined(ta_ref), joined(tb_ref)
    first_t, second_t = first.T, second.T
    folded = jnp.where(row < col, first + first_t, second + second_t)
    on_diagonal = jnp.broadcast_to(group % 7, (TILE, TILE)) == 0
    tt_ref[...] = jnp.where(on_diagonal, folded, first + second_t)
    own = jnp.sum(jnp.where(row == col, first, 0.0), axis=0, keepdims=True)
    targets = tt_ref[pl.ds(pl.multiple_of((y_lo * 2 + core) * ROWS, ROWS), ROWS), :]

    arrived(zf_ref, rz.at[1])
    arrived(zn_ref.at[4], rz.at[2])
    total = total + zf_ref[0] + zf_ref[1] + zn_ref[4]
    piece_ref[...] = 2.0 * jax.nn.sigmoid(total) - targets
    for i, (dx, dy) in enumerate(OFFSETS):
        copy(piece_ref, o_ref.at[core, mine], s3, r3.at[i], device(dx, dy)).start()
    copy(piece_ref, o_ref.at[core, mine], s4, r4, partner).start()
    o_ref[core, mine] = piece_ref[...]

    @pl.when(owner)
    def _():
        arrived(ef_ref, er.at[2])
        arrived(en_ref.at[4], er.at[3])
        acc = ez_ref[1] + ef_ref[0] + ef_ref[1] + en_ref[4]
        ep_ref[...] = 2.0 * jax.nn.sigmoid(acc) - 2.0 * own
        for dx, dy in OFFSETS:
            copy(ep_ref, eo_ref.at[core], es.at[3], er.at[4], device(dx, dy)).start()
        copy(ep_ref, eo_ref.at[core], es.at[4], er.at[5], partner).start()
        eo_ref[core] = ep_ref[...]

    for i in reversed(range(15)):
        dx, dy = OFFSETS[i]
        piece = o_ref.at[core, place(-dx, -dy)]
        arrived(piece, r3.at[i])
        copy(piece, piece, s4, r4, partner).start()

    @pl.when(jnp.logical_not(owner))
    def _():
        arrived(eo_ref.at[core], er.at[4])
        copy(eo_ref.at[core], eo_ref.at[core], es.at[4], er.at[5], partner).start()

    arrived(o_ref.at[other], r4)
    arrived(eo_ref.at[other], er.at[5])
    unpack(o_ref, eo_ref, s_ref)

    left(a_ref, s0)
    left(y_ref, s1)
    left(zn_ref, sz.at[0])
    left(zf_ref, sz.at[1])
    left(t_ref.at[pl.ds(0, 15)], st.at[0])
    left(ta_ref.at[core], st.at[1])
    left(tb_ref, st.at[2])
    left(b_ref, s3)
    left(o_ref.at[core], s4)
    left(ep_ref, es.at[4])

    @pl.when(owner)
    def _():
        left(en_ref, es.at[1])
        left(ef_ref, es.at[2])
        left(eb_ref.at[pl.ds(0, 15)], es.at[3])

    @pl.when(jnp.logical_not(owner))
    def _():
        left(ey_ref, es.at[0])


def back_kernel(w_ref, qt_ref, qk_ref, p_ref, s_ref, rb_ref, rr_ref, qg_hbm, kg_hbm, wg_ref, d_ref, ds_ref, qg_ref, kg_ref, sems):
    scale = DH ** (-0.5)
    chunk = 32
    zero = jnp.zeros((8, L), F32)

    def gather(i, carry):
        rows = pl.ds(pl.multiple_of(i * chunk, chunk), chunk)
        s = s_ref[rows, :]
        out = []
        for layer in range(2):
            wide = jnp.concatenate([rb_ref[layer, rows, :]] * 4, axis=1)
            prod = s * wide
            acc = carry[layer]
            for t in range(chunk // 8):
                acc = acc + prod[t * 8 : (t + 1) * 8, :]
            out.append(acc)
        return tuple(out)

    sums = lax.fori_loop(0, L // chunk, gather, (zero, zero), unroll=2)
    grads = []
    stores = []
    for layer in range(2):
        h_row = jnp.sum(sums[layer], axis=0, keepdims=True)
        quad = jnp.sum(h_row * rr_ref[layer : layer + 1, :], axis=1, keepdims=True)
        h_scaled = h_row * (1.0 / TOTAL)
        d_row = quad * (1.0 / (TOTAL * TOTAL)) - h_scaled
        for t in range(4):
            wide = jnp.broadcast_to(d_row[:, t * TILE : (t + 1) * TILE], (TILE, TILE))
            d_ref[layer, t * TILE : (t + 1) * TILE, :] = wide.T
        acc = zero
        for i in range(L // chunk):
            rows = slice(i * chunk, (i + 1) * chunk)
            s = s_ref[rows, :]
            probs = p_ref[layer, rows, :]
            wide = jnp.concatenate([d_ref[layer, rows, :]] * 4, axis=1)
            dprobs = s + wide - h_scaled
            prod = probs * s
            for t in range(chunk // 8):
                acc = acc + prod[t * 8 : (t + 1) * 8, :]
            inner = jnp.sum(probs * dprobs, axis=1, keepdims=True)
            ds_ref[layer, rows, :] = (probs * (dprobs - inner)).astype(BF16)
        grads.append(jnp.sum(jnp.sum(acc, axis=0, keepdims=True), axis=1, keepdims=True) - quad * (0.5 / TOTAL))
        factor = w_ref[layer : layer + 1, :] * scale
        qg = jnp.dot(ds_ref[layer], qk_ref[layer, 1], preferred_element_type=F32)
        qg_ref[layer] = (qg * factor).astype(BF16)
        stores.append(pltpu.make_async_copy(qg_ref.at[layer], qg_hbm.at[layer], sems.at[2 * layer]))
        stores[-1].start()
        kg = jnp.dot(qt_ref[layer], ds_ref[layer], preferred_element_type=F32)
        kg_ref[layer] = (kg.T * factor).astype(BF16)
        stores.append(pltpu.make_async_copy(kg_ref.at[layer], kg_hbm.at[layer], sems.at[2 * layer + 1]))
        stores[-1].start()
    lane = lax.broadcasted_iota(jnp.int32, (1, 2), 1)
    wg_ref[...] = jnp.where(lane == 0, grads[0], grads[1])
    for c in stores:
        c.wait()


def vmem():
    return pl.BlockSpec(memory_space=pltpu.VMEM)


def smem():
    return pl.BlockSpec(memory_space=pltpu.SMEM)


def hbm():
    return pl.BlockSpec(memory_space=pltpu.HBM)


def on_device(queries, keys, head_weight, slot_head, target):
    q = queries.reshape(2, L, DH)
    k = keys.reshape(2, L, DH)
    dma = pltpu.SemaphoreType.DMA
    probs, s_map, rb, rr, w, qk, q_turned = pl.pallas_call(
        exchange_kernel,
        out_shape=(
            pltpu.VMEM((2, L, L), F32),
            pltpu.VMEM((L, L), F32),
            pltpu.VMEM((2, L, TILE), F32),
            pltpu.VMEM((2, L), F32),
            pltpu.VMEM((2, TILE), F32),
            pltpu.VMEM((2, 2, L, DH), BF16),
            pltpu.VMEM((2, DH, L), BF16),
        ),
        in_specs=[smem()] + [hbm()] * 4,
        out_specs=(vmem(),) * 7,
        scratch_shapes=[
            pltpu.VMEM((2, 40), F32),
            pltpu.VMEM((8, L), jnp.int32),
            pltpu.VMEM((L, L), F32),
            pltpu.VMEM((2, 16, ROWS, TILE), F32),
            pltpu.VMEM((16 * ROWS + 8, TILE), F32),
            pltpu.VMEM((15, ROWS, TILE), F32),
            pltpu.VMEM((15, ROWS, TILE), F32),
            pltpu.VMEM((2, ROWS, TILE), F32),
            pltpu.VMEM((5, ROWS, TILE), F32),
            pltpu.VMEM((2, ROWS, TILE), F32),
            pltpu.VMEM((16, 8, TILE), jnp.int32),
            pltpu.VMEM((16, 8, TILE), jnp.int32),
            pltpu.VMEM((2, 8, 8, TILE), jnp.int32),
            pltpu.VMEM((2, 8, 8, TILE), jnp.int32),
            pltpu.VMEM((TILE, TILE), F32),
            pltpu.VMEM((ROWS, TILE), F32),
            pltpu.VMEM((2, 16, ROWS, TILE), F32),
            pltpu.VMEM((2, 8, TILE), F32),
            pltpu.VMEM((8, TILE), F32),
            pltpu.VMEM((16, 8, TILE), F32),
            pltpu.VMEM((2, 8, TILE), F32),
            pltpu.VMEM((5, 8, TILE), F32),
            pltpu.VMEM((2, 8, TILE), F32),
            pltpu.VMEM((8, TILE), F32),
            pltpu.VMEM((2, 8, TILE), F32),
            dma((4,)), dma, dma((4,)), dma, dma, dma((2,)), dma((3,)), dma((3,)), dma((4,)),
            dma, dma((15,)), dma, dma, dma((5,)), dma((6,)),
        ],
        compiler_params=pltpu.CompilerParams(collective_id=0, has_side_effects=True, vmem_limit_bytes=16 << 20),
    )(slot_head, *[pltpu.with_memory_space_constraint(v, pltpu.HBM) for v in (head_weight, target, q, k)])
    qg, kg, wg = pl.pallas_call(
        back_kernel,
        out_shape=(
            jax.ShapeDtypeStruct((2, L, DH), BF16),
            jax.ShapeDtypeStruct((2, L, DH), BF16),
            jax.ShapeDtypeStruct((1, 2), F32),
        ),
        in_specs=[vmem()] * 7,
        out_specs=(hbm(), hbm(), vmem()),
        scratch_shapes=[
            pltpu.VMEM((2, L, TILE), F32),
            pltpu.VMEM((2, L, L), BF16),
            pltpu.VMEM((2, L, DH), BF16),
            pltpu.VMEM((2, L, DH), BF16),
            pltpu.SemaphoreType.DMA((4,)),
        ],
        compiler_params=pltpu.CompilerParams(vmem_limit_bytes=16 << 20),
    )(w, q_turned, qk, probs, s_map, rb, rr)
    return (qg.reshape(2, 1, L, DH), kg.reshape(2, 1, L, DH), wg.reshape(2, 1))


def solution(mesh):
    placed = (
        P("layer", "head", None, None),
        P("layer", "head", None, None),
        P("layer", None),
        P("head"),
        P("head", None),
    )
    return jax.shard_map(
        on_device,
        mesh=mesh,
        in_specs=placed,
        out_specs=(P("layer", "head", None, None), P("layer", "head", None, None), P("layer", "head")),
        check_vma=False,
    )
```

```python
import jax
import jax.numpy as jnp
from jax import lax
from jax.experimental import pallas as pl
from jax.experimental.pallas import tpu as pltpu
from jax.sharding import PartitionSpec as P

MESH = pl.DeviceIdType.MESH
F32 = jnp.float32
BF16 = jnp.bfloat16
L = 512
DH = 128
TILE = 128
TOTAL = 2.0 * L
OFF = {1: (0, 1), 2: (0, 2), 3: (1, 3), 4: (3, 0), 5: (2, 1), 6: (3, 2)}
DIAG = {0: (0, 1), 7: (3, 2)}
KEEP = (0, 0, 0, 1, 1, 0, 1, 1)
MIRROR = (1, 0, 5, 4, 2, 3, 7, 6)
MIRRORED = (1, 0, 4, 5, 3, 2, 7, 6)
ROWS = 32
OFFSETS = sorted(
    ((dx, dy) for dx in range(4) for dy in range(4) if dx or dy),
    key=lambda o: -(min(o[0], 4 - o[0]) + min(o[1], 4 - o[1])),
)

GROUPS = (0,) * 5 + (1,) * 3 + (2,) * 3 + (3,) * 4


def pick(index, table):
    value = jnp.int32(table[0])
    for k in range(1, len(table)):
        value = jnp.where(index == k, jnp.int32(table[k]), value)
    return value


def slot_weights(slot_ref, hw_ref):
    hw = hw_ref[...]
    lane = lax.broadcasted_iota(jnp.int32, hw.shape, 1)
    return jnp.sum(jnp.where(lane == slot_ref[0], hw, 0.0), axis=1, keepdims=True)


def forward(w, qk_ref, ready, sc_ref, p_ref, rb_ref, rr_ref, x_ref, e_ref):
    scale = DH ** (-0.5)
    chunk = 32
    sums = []
    for layer in range(2):
        ready(layer)
        sc_ref[...] = lax.dot_general(
            qk_ref[layer, 0], qk_ref[layer, 1], (((1,), (1,)), ((), ())), preferred_element_type=F32
        )

        def body(i, csum, layer=layer):
            rows = pl.ds(pl.multiple_of(i * chunk, chunk), chunk)
            scores = sc_ref[rows, :]
            highest = jnp.max(scores, axis=1, keepdims=True)
            expo = jnp.exp((scores - highest) * scale)
            probs = expo * (1.0 / jnp.sum(expo, axis=1, keepdims=True))
            p_ref[layer, rows, :] = probs
            for t in range(chunk // 8):
                csum = csum + probs[t * 8 : (t + 1) * 8, :]
            return csum

        csum = lax.fori_loop(0, L // chunk, body, jnp.zeros((8, L), F32), unroll=16)
        rowsum = 1.0 + jnp.sum(csum, axis=0, keepdims=True)
        rr_ref[layer : layer + 1, :] = rowsum
        for t in range(4):
            wide = jnp.broadcast_to(rowsum[:, t * TILE : (t + 1) * TILE], (TILE, TILE))
            rb_ref[layer, t * TILE : (t + 1) * TILE, :] = wide.T
        sums.append(rowsum * (w[layer : layer + 1, 0:1] / TOTAL))

    def cut(t):
        return slice(t * TILE, (t + 1) * TILE)

    def half(a, b):
        return w[0:1, :] * p_ref[0, cut(a), cut(b)] + w[1:2, :] * p_ref[1, cut(a), cut(b)]

    def block(a, b):
        outer = rb_ref[0, cut(a), :] * sums[0][:, cut(b)] + rb_ref[1, cut(a), :] * sums[1][:, cut(b)]
        return half(a, b) + half(b, a).T - outer

    row = lax.broadcasted_iota(jnp.int32, (TILE, TILE), 0)
    col = lax.broadcasted_iota(jnp.int32, (TILE, TILE), 1)
    for g in range(8):
        if g in OFF:
            full = block(*OFF[g])
        else:
            upper = block(DIAG[g][0], DIAG[g][0])
            full = jnp.where(row < col, upper, block(DIAG[g][1], DIAG[g][1]))
            extra = jnp.sum(jnp.where(row == col, upper, 0.0), axis=0, keepdims=True)
            e_ref[g // 7] = jnp.broadcast_to(extra, (8, TILE))
        for part in range(4):
            x_ref[part % 2, 2 * g + part // 2] = full[part * ROWS : (part + 1) * ROWS, :]


def unpack(o_ref, eo_ref, s_ref):
    row = lax.broadcasted_iota(jnp.int32, (TILE, TILE), 0)
    col = lax.broadcasted_iota(jnp.int32, (TILE, TILE), 1)

    def cut(t):
        return slice(t * TILE, (t + 1) * TILE)

    for g in range(8):
        full = jnp.concatenate([o_ref[part % 2, 2 * g + part // 2] for part in range(4)], axis=0)
        if g in OFF:
            a, b = OFF[g]
            s_ref[cut(a), cut(b)] = full
            s_ref[cut(b), cut(a)] = full.T
        else:
            a, b = DIAG[g]
            turned = full.T
            diagonal = eo_ref[g // 7, 0:1, :]
            upper = jnp.where(row < col, full, jnp.where(row == col, diagonal, turned))
            s_ref[cut(a), cut(a)] = upper
            s_ref[cut(b), cut(b)] = jnp.where(row < col, turned, full)


def exchange_kernel(
    slot_ref, hw_hbm, target_hbm, q_hbm, k_hbm,
    p_ref, s_ref, rb_ref, rr_ref, w_ref, qk_ref, qt_ref,
    hw_ref, target_ref, sc_ref, x_ref, a_ref, y_ref, b_ref, z_ref, zn_ref, zf_ref,
    tn_ref, t_ref, to_ref, ta_ref, tb_ref, tt_ref, piece_ref, o_ref,
    e_ref, ey_ref, eb_ref, ez_ref, en_ref, ef_ref, ep_ref, eo_ref,
    sin, s0, r0, s1, r1, sz, rz, st, rt, s3, r3, s4, r4, es, er, relay,
):
    loads = [
        pltpu.make_async_copy(q_hbm.at[0], qk_ref.at[0, 0], sin.at[0]),
        pltpu.make_async_copy(k_hbm.at[0], qk_ref.at[0, 1], sin.at[0]),
        pltpu.make_async_copy(hw_hbm, hw_ref, sin.at[2]),
        pltpu.make_async_copy(q_hbm.at[1], qk_ref.at[1, 0], sin.at[1]),
        pltpu.make_async_copy(k_hbm.at[1], qk_ref.at[1, 1], sin.at[1]),
        pltpu.make_async_copy(target_hbm, target_ref, sin.at[3]),
    ]
    for c in loads:
        c.start()
    layer_pos = lax.axis_index("layer")
    head_pos = lax.axis_index("head")
    x = layer_pos % 4
    y_lo = layer_pos // 4
    core = head_pos % 2
    z = (head_pos // 2) % 16
    y_hi = head_pos // 32
    y = y_hi * 2 + y_lo
    group = y_hi * 4 + x
    other = 1 - core
    mine = group * 2 + y_lo
    sign = 1 - 2 * core

    def device(dx=0, dy=0, dz=0, flip=False):
        nx = (x + dx) % 4
        ny = (y + dy) % 4
        nz = (z + sign * dz + 16) % 16
        nc = other if flip else core
        return {"layer": (ny % 2) * 4 + nx, "head": (ny // 2) * 32 + nz * 2 + nc}

    def place(dx, dy):
        nx = (x + dx) % 4
        ny = (y + dy) % 4
        return ((ny // 2) * 4 + nx) * 2 + ny % 2

    def in_group(g, c):
        return {"layer": y_lo * 4 + g % 4, "head": (g // 4) * 32 + z * 2 + c}

    partner = device(flip=True)
    sent_to = pick(group, MIRROR)
    got_from = pick(group, MIRRORED)

    barrier = pltpu.get_barrier_semaphore()
    greeted = [device(dx, dy) for dx, dy in OFFSETS]
    greeted += [device(dz=d) for d in (3, -3, 2, -2, 1, -1)]
    greeted += [partner, in_group(sent_to, other), in_group(got_from, other)]
    for d in greeted:
        pl.semaphore_signal(barrier, inc=1, device_id=d, device_id_type=MESH)

    def ready(layer):
        pltpu.make_async_copy(qk_ref.at[layer], qk_ref.at[layer], sin.at[layer]).wait()
        if layer == 0:
            loads[2].wait()
            w = slot_weights(slot_ref, hw_ref)
            w_ref[...] = jnp.broadcast_to(w, (2, TILE))

    forward(w_ref, qk_ref, ready, sc_ref, p_ref, rb_ref, rr_ref, x_ref, e_ref)
    loads[5].wait()
    pl.semaphore_wait(barrier, len(greeted))

    def copy(src, dst, ssem, rsem, dev):
        return pltpu.make_async_remote_copy(
            src_ref=src, dst_ref=dst, send_sem=ssem, recv_sem=rsem, device_id=dev, device_id_type=MESH
        )

    def arrived(ref, rsem):
        copy(ref, ref, s0, rsem, partner).wait_recv()

    def left(ref, ssem):
        copy(ref, ref, ssem, r1, partner).wait_send()

    tile = target_ref.at[:, pl.ds(pl.multiple_of(x * TILE, TILE), TILE)]
    for d, slot in ((1, 1), (-1, 3), (2, 0), (-2, 4), (-3, 5)):
        copy(tile, tn_ref.at[slot], st.at[0], rt.at[0], device(dz=d)).start()
    tn_ref[2] = target_ref[:, pl.ds(pl.multiple_of(x * TILE, TILE), TILE)]

    order = OFFSETS + [(0, 0)]
    copy(e_ref.at[other], a_ref.at[pl.ds(16 * ROWS, 8)], s0, r0.at[0], partner).start()
    for i, (dx, dy) in enumerate(order):
        copy(x_ref.at[other, place(dx, dy)], a_ref.at[pl.ds(i * ROWS, ROWS)], s0, r0.at[1 + i // 4], partner).start()

    arrived(a_ref.at[pl.ds(16 * ROWS, 8)], r0.at[0])
    ey_ref[...] = e_ref[core] + a_ref[16 * ROWS : 16 * ROWS + 8, :]
    owner = mine == core * 14
    owner_of_diagonal = {"layer": core * 3, "head": core * 33 + z * 2}

    @pl.when(jnp.logical_not(owner))
    def _():
        copy(ey_ref, eb_ref.at[mine], es.at[0], er.at[0], owner_of_diagonal).start()

    for i, (dx, dy) in enumerate(order):
        if i % 4 == 0:
            arrived(a_ref.at[pl.ds(i * ROWS, 4 * ROWS)], r0.at[1 + i // 4])
        summed = x_ref[core, place(dx, dy)] + a_ref[i * ROWS : (i + 1) * ROWS, :]
        if i < 15:
            y_ref[i] = summed
            copy(y_ref.at[i], b_ref.at[i], s1, r1, device(dx, dy)).start()
        else:
            total = summed

    arrived(t_ref.at[pl.ds(0, 5)], rt.at[0])
    pl.semaphore_signal(relay, inc=1, device_id=device(dz=-5), device_id_type=MESH)
    copy(tn_ref.at[pl.ds(0, 5)], t_ref.at[pl.ds(0, 5)], st.at[0], rt.at[1], device(dz=5)).start()
    copy(tn_ref, t_ref.at[pl.ds(10, 6)], st.at[0], rt.at[1], device(dz=-5)).start()

    arrived(b_ref, r1)
    for i in range(15):
        total = total + b_ref[i]
    z_ref[0] = total
    near = (1, -1, 2, -2)
    for i, d in enumerate(near):
        copy(z_ref.at[0], zn_ref.at[i], sz.at[0], rz.at[0], device(dz=d)).start()
    pl.semaphore_wait(relay, 1)
    copy(z_ref.at[0], zn_ref.at[4], sz.at[0], rz.at[2], device(dz=8)).start()

    @pl.when(owner)
    def _():
        eb_ref[mine] = ey_ref[...]
        arrived(eb_ref.at[pl.ds(0, 15)], er.at[0])
        acc = eb_ref[0]
        for i in range(1, 16):
            acc = acc + eb_ref[i]
        ez_ref[0] = acc
        for i, d in enumerate(near):
            copy(ez_ref.at[0], en_ref.at[i], es.at[1], er.at[1], device(dz=d)).start()
        copy(ez_ref.at[0], en_ref.at[4], es.at[1], er.at[3], device(dz=8)).start()

    arrived(zn_ref.at[pl.ds(0, 4)], rz.at[0])
    for i in range(4):
        total = total + zn_ref[i]
    z_ref[1] = total
    for i, d in enumerate((5, -5)):
        copy(z_ref.at[1], zf_ref.at[i], sz.at[1], rz.at[1], device(dz=d)).start()

    @pl.when(owner)
    def _():
        arrived(en_ref.at[pl.ds(0, 4)], er.at[1])
        acc = ez_ref[0]
        for i in range(4):
            acc = acc + en_ref[i]
        ez_ref[1] = acc
        for i, d in enumerate((5, -5)):
            copy(ez_ref.at[1], ef_ref.at[i], es.at[2], er.at[2], device(dz=d)).start()

    arrived(t_ref.at[pl.ds(0, 11)], rt.at[1])
    for slot in range(16):
        to_ref[(z + sign * (slot - 7) + 16) % 16] = tn_ref[slot - 5] if 5 <= slot < 10 else t_ref[slot]
    keep = pick(group, KEEP)
    kept = to_ref.at[pl.ds(keep * 8, 8)]
    given = to_ref.at[pl.ds((1 - keep) * 8, 8)]
    copy(kept, ta_ref.at[core], st.at[1], rt.at[2], partner).start()
    copy(given, tb_ref.at[core], st.at[2], rt.at[3], in_group(sent_to, core)).start()
    copy(given, tb_ref.at[core], st.at[2], rt.at[3], in_group(sent_to, other)).start()
    ta_ref[core] = to_ref[pl.ds(keep * 8, 8)]
    for layer in range(2):
        qt_ref[layer] = qk_ref[layer, 0].astype(F32).T.astype(BF16)

    arrived(ta_ref.at[other], rt.at[2])
    arrived(tb_ref, rt.at[3])

    def joined(ref):
        return jnp.concatenate([ref[t % 2, t // 2] for t in range(16)], axis=0).astype(F32)

    row = lax.broadcasted_iota(jnp.int32, (TILE, TILE), 0)
    col = lax.broadcasted_iota(jnp.int32, (TILE, TILE), 1)
    first, second = joined(ta_ref), joined(tb_ref)
    first_t, second_t = first.T, second.T
    folded = jnp.where(row < col, first + first_t, second + second_t)
    on_diagonal = jnp.broadcast_to(group % 7, (TILE, TILE)) == 0
    tt_ref[...] = jnp.where(on_diagonal, folded, first + second_t)
    own = jnp.sum(jnp.where(row == col, first, 0.0), axis=0, keepdims=True)
    targets = tt_ref[pl.ds(pl.multiple_of((y_lo * 2 + core) * ROWS, ROWS), ROWS), :]

    arrived(zf_ref, rz.at[1])
    arrived(zn_ref.at[4], rz.at[2])
    total = total + zf_ref[0] + zf_ref[1] + zn_ref[4]
    piece_ref[...] = 2.0 * jax.nn.sigmoid(total) - targets
    for i, (dx, dy) in enumerate(OFFSETS):
        copy(piece_ref, o_ref.at[core, mine], s3, r3.at[GROUPS[i]], device(dx, dy)).start()
    copy(piece_ref, o_ref.at[core, mine], s4, r4, partner).start()
    o_ref[core, mine] = piece_ref[...]

    @pl.when(owner)
    def _():
        arrived(ef_ref, er.at[2])
        arrived(en_ref.at[4], er.at[3])
        acc = ez_ref[1] + ef_ref[0] + ef_ref[1] + en_ref[4]
        ep_ref[...] = 2.0 * jax.nn.sigmoid(acc) - 2.0 * own
        for dx, dy in OFFSETS:
            copy(ep_ref, eo_ref.at[core], es.at[3], er.at[4], device(dx, dy)).start()
        copy(ep_ref, eo_ref.at[core], es.at[4], er.at[5], partner).start()
        eo_ref[core] = ep_ref[...]

    for g in (3, 2, 1, 0):
        members = [i for i in range(15) if GROUPS[i] == g]
        arrived(y_ref.at[pl.ds(0, len(members))], r3.at[g])
        for i in members:
            dx, dy = OFFSETS[i]
            piece = o_ref.at[core, place(-dx, -dy)]
            copy(piece, piece, s4, r4, partner).start()

    @pl.when(jnp.logical_not(owner))
    def _():
        arrived(eo_ref.at[core], er.at[4])
        copy(eo_ref.at[core], eo_ref.at[core], es.at[4], er.at[5], partner).start()

    arrived(o_ref.at[other], r4)
    arrived(eo_ref.at[other], er.at[5])
    unpack(o_ref, eo_ref, s_ref)

    left(a_ref, s0)
    left(b_ref, s1)
    left(zn_ref, sz.at[0])
    left(zf_ref, sz.at[1])
    left(t_ref, st.at[0])
    left(ta_ref.at[core], st.at[1])
    left(tb_ref, st.at[2])
    left(b_ref, s3)
    left(o_ref.at[core], s4)
    left(ep_ref, es.at[4])

    @pl.when(owner)
    def _():
        left(en_ref, es.at[1])
        left(ef_ref, es.at[2])
        left(eb_ref.at[pl.ds(0, 15)], es.at[3])

    @pl.when(jnp.logical_not(owner))
    def _():
        left(ey_ref, es.at[0])


def back_kernel(w_ref, qt_ref, qk_ref, p_ref, s_ref, rb_ref, rr_ref, qg_hbm, kg_hbm, wg_ref, d_ref, ds_ref, qg_ref, kg_ref, sems):
    scale = DH ** (-0.5)
    chunk = 32
    zero = jnp.zeros((8, L), F32)

    def gather(i, carry):
        rows = pl.ds(pl.multiple_of(i * chunk, chunk), chunk)
        s = s_ref[rows, :]
        out = []
        for layer in range(2):
            wide = jnp.concatenate([rb_ref[layer, rows, :]] * 4, axis=1)
            prod = s * wide
            acc = carry[layer]
            for t in range(chunk // 8):
                acc = acc + prod[t * 8 : (t + 1) * 8, :]
            out.append(acc)
        return tuple(out)

    sums = lax.fori_loop(0, L // chunk, gather, (zero, zero), unroll=2)
    grads = []
    stores = []
    h_rows = []
    for layer in range(2):
        h_row = jnp.sum(sums[layer], axis=0, keepdims=True)
        quad = jnp.sum(h_row * rr_ref[layer : layer + 1, :], axis=1, keepdims=True)
        h_scaled = h_row * (1.0 / TOTAL)
        d_row = quad * (1.0 / (TOTAL * TOTAL)) - h_scaled
        for t in range(4):
            wide = jnp.broadcast_to(d_row[:, t * TILE : (t + 1) * TILE], (TILE, TILE))
            d_ref[layer, t * TILE : (t + 1) * TILE, :] = wide.T
        h_rows.append(h_scaled)
        grads.append(-quad * (0.5 / TOTAL))

    def map_rows(layer, i, acc):
        rows = slice(i * chunk, (i + 1) * chunk)
        s = s_ref[rows, :]
        probs = p_ref[layer, rows, :]
        wide = jnp.concatenate([d_ref[layer, rows, :]] * 4, axis=1)
        dprobs = s + wide - h_rows[layer]
        prod = probs * s
        for t in range(chunk // 8):
            acc = acc + prod[t * 8 : (t + 1) * 8, :]
        inner = jnp.sum(probs * dprobs, axis=1, keepdims=True)
        ds_ref[layer, rows, :] = (probs * (dprobs - inner)).astype(BF16)
        return acc

    def query_rows(layer, i, count):
        rows = slice(i * count, (i + 1) * count)
        qg = jnp.dot(ds_ref[layer, rows, :], qk_ref[layer, 1], preferred_element_type=F32)
        qg_ref[layer, rows, :] = (qg * (w_ref[layer : layer + 1, :] * scale)).astype(BF16)

    def key_rows(layer, i, count):
        rows = slice(i * count, (i + 1) * count)
        kg = jnp.dot(qt_ref[layer], ds_ref[layer, :, rows], preferred_element_type=F32)
        kg_ref[layer, rows, :] = (kg.T * (w_ref[layer : layer + 1, :] * scale)).astype(BF16)

    def store(src, dst, index):
        stores.append(pltpu.make_async_copy(src, dst, sems.at[index]))
        stores[-1].start()

    acc = zero
    for i in range(16):
        acc = map_rows(0, i, acc)
    grads[0] = grads[0] + jnp.sum(jnp.sum(acc, axis=0, keepdims=True), axis=1, keepdims=True)
    acc = zero
    for i in range(16):
        acc = map_rows(1, i, acc)
        if i % 8 == 3:
            query_rows(0, i // 8, 256)
        if i % 8 == 7:
            key_rows(0, i // 8, 256)
    grads[1] = grads[1] + jnp.sum(jnp.sum(acc, axis=0, keepdims=True), axis=1, keepdims=True)
    store(qg_ref.at[0], qg_hbm.at[0], 0)
    store(kg_ref.at[0], kg_hbm.at[0], 1)
    for i in range(2):
        key_rows(1, i, 256)
    store(kg_ref.at[1], kg_hbm.at[1], 2)
    for i in range(2):
        query_rows(1, i, 256)
    store(qg_ref.at[1], qg_hbm.at[1], 3)
    lane = lax.broadcasted_iota(jnp.int32, (1, 2), 1)
    wg_ref[...] = jnp.where(lane == 0, grads[0], grads[1])
    for c in stores:
        c.wait()


def vmem():
    return pl.BlockSpec(memory_space=pltpu.VMEM)


def smem():
    return pl.BlockSpec(memory_space=pltpu.SMEM)


def hbm():
    return pl.BlockSpec(memory_space=pltpu.HBM)


def on_device(queries, keys, head_weight, slot_head, target):
    q = queries.reshape(2, L, DH)
    k = keys.reshape(2, L, DH)
    dma = pltpu.SemaphoreType.DMA
    probs, s_map, rb, rr, w, qk, q_turned = pl.pallas_call(
        exchange_kernel,
        out_shape=(
            pltpu.VMEM((2, L, L), F32),
            pltpu.VMEM((L, L), F32),
            pltpu.VMEM((2, L, TILE), F32),
            pltpu.VMEM((2, L), F32),
            pltpu.VMEM((2, TILE), F32),
            pltpu.VMEM((2, 2, L, DH), BF16),
            pltpu.VMEM((2, DH, L), BF16),
        ),
        in_specs=[smem()] + [hbm()] * 4,
        out_specs=(vmem(),) * 7,
        scratch_shapes=[
            pltpu.VMEM((2, 40), F32),
            pltpu.VMEM((8, L), jnp.int32),
            pltpu.VMEM((L, L), F32),
            pltpu.VMEM((2, 16, ROWS, TILE), F32),
            pltpu.VMEM((16 * ROWS + 8, TILE), F32),
            pltpu.VMEM((15, ROWS, TILE), F32),
            pltpu.VMEM((15, ROWS, TILE), F32),
            pltpu.VMEM((3, ROWS, TILE), F32),
            pltpu.VMEM((5, ROWS, TILE), F32),
            pltpu.VMEM((2, ROWS, TILE), F32),
            pltpu.VMEM((6, 8, TILE), jnp.int32),
            pltpu.VMEM((16, 8, TILE), jnp.int32),
            pltpu.VMEM((16, 8, TILE), jnp.int32),
            pltpu.VMEM((2, 8, 8, TILE), jnp.int32),
            pltpu.VMEM((2, 8, 8, TILE), jnp.int32),
            pltpu.VMEM((TILE, TILE), F32),
            pltpu.VMEM((ROWS, TILE), F32),
            pltpu.VMEM((2, 16, ROWS, TILE), F32),
            pltpu.VMEM((2, 8, TILE), F32),
            pltpu.VMEM((8, TILE), F32),
            pltpu.VMEM((16, 8, TILE), F32),
            pltpu.VMEM((3, 8, TILE), F32),
            pltpu.VMEM((5, 8, TILE), F32),
            pltpu.VMEM((2, 8, TILE), F32),
            pltpu.VMEM((8, TILE), F32),
            pltpu.VMEM((2, 8, TILE), F32),
            dma((4,)), dma, dma((5,)), dma, dma, dma((2,)), dma((3,)), dma((3,)), dma((4,)),
            dma, dma((4,)), dma, dma, dma((5,)), dma((6,)), pltpu.SemaphoreType.REGULAR,
        ],
        compiler_params=pltpu.CompilerParams(collective_id=0, has_side_effects=True, vmem_limit_bytes=16 << 20),
    )(slot_head, *[pltpu.with_memory_space_constraint(v, pltpu.HBM) for v in (head_weight, target, q, k)])
    qg, kg, wg = pl.pallas_call(
        back_kernel,
        out_shape=(
            jax.ShapeDtypeStruct((2, L, DH), BF16),
            jax.ShapeDtypeStruct((2, L, DH), BF16),
            jax.ShapeDtypeStruct((1, 2), F32),
        ),
        in_specs=[vmem()] * 7,
        out_specs=(hbm(), hbm(), vmem()),
        scratch_shapes=[
            pltpu.VMEM((2, L, TILE), F32),
            pltpu.VMEM((2, L, L), BF16),
            pltpu.VMEM((2, L, DH), BF16),
            pltpu.VMEM((2, L, DH), BF16),
            pltpu.SemaphoreType.DMA((4,)),
        ],
        compiler_params=pltpu.CompilerParams(vmem_limit_bytes=16 << 20),
    )(w, q_turned, qk, probs, s_map, rb, rr)
    return (qg.reshape(2, 1, L, DH), kg.reshape(2, 1, L, DH), wg.reshape(2, 1))


def solution(mesh):
    placed = (
        P("layer", "head", None, None),
        P("layer", "head", None, None),
        P("layer", None),
        P("head"),
        P("head", None),
    )
    return jax.shard_map(
        on_device,
        mesh=mesh,
        in_specs=placed,
        out_specs=(P("layer", "head", None, None), P("layer", "head", None, None), P("layer", "head")),
        check_vma=False,
    )
```

```python
import jax
import jax.numpy as jnp
from jax import lax
from jax.experimental import pallas as pl
from jax.experimental.pallas import tpu as pltpu
from jax.sharding import PartitionSpec as P

MESH = pl.DeviceIdType.MESH
F32 = jnp.float32
BF16 = jnp.bfloat16
L = 512
DH = 128
TILE = 128
TOTAL = 2.0 * L
OFF = {1: (0, 1), 2: (0, 2), 3: (1, 3), 4: (3, 0), 5: (2, 1), 6: (3, 2)}
DIAG = {0: (0, 1), 7: (3, 2)}
KEEP = (0, 0, 0, 1, 1, 0, 1, 1)
MIRROR = (1, 0, 5, 4, 2, 3, 7, 6)
MIRRORED = (1, 0, 4, 5, 3, 2, 7, 6)
ROWS = 32
OFFSETS = sorted(
    ((dx, dy) for dx in range(4) for dy in range(4) if dx or dy),
    key=lambda o: -(min(o[0], 4 - o[0]) + min(o[1], 4 - o[1])),
)


def pick(index, table):
    value = jnp.int32(table[0])
    for k in range(1, len(table)):
        value = jnp.where(index == k, jnp.int32(table[k]), value)
    return value


def slot_weights(slot_ref, hw_ref):
    hw = hw_ref[...]
    lane = lax.broadcasted_iota(jnp.int32, hw.shape, 1)
    return jnp.sum(jnp.where(lane == slot_ref[0], hw, 0.0), axis=1, keepdims=True)


def forward(w, qk_ref, ready, sc_ref, p_ref, rb_ref, rr_ref, x_ref, e_ref):
    scale = DH ** (-0.5)
    chunk = 32
    sums = []
    for layer in range(2):
        ready(layer)
        sc_ref[layer] = lax.dot_general(
            qk_ref[layer, 0], qk_ref[layer, 1], (((1,), (1,)), ((), ())), preferred_element_type=F32
        )
    for layer in range(2):

        def body(i, csum, layer=layer):
            rows = pl.ds(pl.multiple_of(i * chunk, chunk), chunk)
            scores = sc_ref[layer, rows, :]
            highest = jnp.max(scores, axis=1, keepdims=True)
            expo = jnp.exp((scores - highest) * scale)
            probs = expo * (1.0 / jnp.sum(expo, axis=1, keepdims=True))
            p_ref[layer, rows, :] = probs
            for t in range(chunk // 8):
                csum = csum + probs[t * 8 : (t + 1) * 8, :]
            return csum

        csum = lax.fori_loop(0, L // chunk, body, jnp.zeros((8, L), F32), unroll=16)
        rowsum = 1.0 + jnp.sum(csum, axis=0, keepdims=True)
        rr_ref[layer : layer + 1, :] = rowsum
        for t in range(4):
            wide = jnp.broadcast_to(rowsum[:, t * TILE : (t + 1) * TILE], (TILE, TILE))
            rb_ref[layer, t * TILE : (t + 1) * TILE, :] = wide.T
        sums.append(rowsum * (w[layer : layer + 1, 0:1] / TOTAL))

    def cut(t):
        return slice(t * TILE, (t + 1) * TILE)

    def half(a, b):
        return w[0:1, :] * p_ref[0, cut(a), cut(b)] + w[1:2, :] * p_ref[1, cut(a), cut(b)]

    def block(a, b):
        outer = rb_ref[0, cut(a), :] * sums[0][:, cut(b)] + rb_ref[1, cut(a), :] * sums[1][:, cut(b)]
        return half(a, b) + half(b, a).T - outer

    row = lax.broadcasted_iota(jnp.int32, (TILE, TILE), 0)
    col = lax.broadcasted_iota(jnp.int32, (TILE, TILE), 1)
    for g in range(8):
        if g in OFF:
            full = block(*OFF[g])
        else:
            upper = block(DIAG[g][0], DIAG[g][0])
            full = jnp.where(row < col, upper, block(DIAG[g][1], DIAG[g][1]))
            extra = jnp.sum(jnp.where(row == col, upper, 0.0), axis=0, keepdims=True)
            e_ref[g // 7] = jnp.broadcast_to(extra, (8, TILE))
        for part in range(4):
            x_ref[part % 2, 2 * g + part // 2] = full[part * ROWS : (part + 1) * ROWS, :]


def unpack(o_ref, eo_ref, s_ref):
    row = lax.broadcasted_iota(jnp.int32, (TILE, TILE), 0)
    col = lax.broadcasted_iota(jnp.int32, (TILE, TILE), 1)

    def cut(t):
        return slice(t * TILE, (t + 1) * TILE)

    for g in range(8):
        full = jnp.concatenate([o_ref[part % 2, 2 * g + part // 2] for part in range(4)], axis=0)
        if g in OFF:
            a, b = OFF[g]
            s_ref[cut(a), cut(b)] = full
            s_ref[cut(b), cut(a)] = full.T
        else:
            a, b = DIAG[g]
            turned = full.T
            diagonal = eo_ref[g // 7, 0:1, :]
            upper = jnp.where(row < col, full, jnp.where(row == col, diagonal, turned))
            s_ref[cut(a), cut(a)] = upper
            s_ref[cut(b), cut(b)] = jnp.where(row < col, turned, full)


def exchange_kernel(
    slot_ref, hw_hbm, target_hbm, q_hbm, k_hbm,
    p_ref, s_ref, rb_ref, rr_ref, w_ref, qk_ref, qt_ref,
    hw_ref, target_ref, sc_ref, x_ref, a_ref, y_ref, b_ref, z_ref, zn_ref, zf_ref,
    tn_ref, t_ref, to_ref, ta_ref, tb_ref, tt_ref, piece_ref, o_ref,
    e_ref, ey_ref, eb_ref, ez_ref, en_ref, ef_ref, ep_ref, eo_ref,
    sin, s0, r0, s1, r1, sz, rz, st, rt, s3, r3, s4, r4, es, er, relay,
):
    loads = [
        pltpu.make_async_copy(q_hbm.at[0], qk_ref.at[0, 0], sin.at[0]),
        pltpu.make_async_copy(k_hbm.at[0], qk_ref.at[0, 1], sin.at[0]),
        pltpu.make_async_copy(hw_hbm, hw_ref, sin.at[2]),
        pltpu.make_async_copy(q_hbm.at[1], qk_ref.at[1, 0], sin.at[1]),
        pltpu.make_async_copy(k_hbm.at[1], qk_ref.at[1, 1], sin.at[1]),
        pltpu.make_async_copy(target_hbm, target_ref, sin.at[3]),
    ]
    for c in loads:
        c.start()
    layer_pos = lax.axis_index("layer")
    head_pos = lax.axis_index("head")
    x = layer_pos % 4
    y_lo = layer_pos // 4
    core = head_pos % 2
    z = (head_pos // 2) % 16
    y_hi = head_pos // 32
    y = y_hi * 2 + y_lo
    group = y_hi * 4 + x
    other = 1 - core
    mine = group * 2 + y_lo
    sign = 1 - 2 * core

    def device(dx=0, dy=0, dz=0, flip=False):
        nx = (x + sign * dx + 4) % 4
        ny = (y + sign * dy + 4) % 4
        nz = (z + sign * dz + 16) % 16
        nc = other if flip else core
        return {"layer": (ny % 2) * 4 + nx, "head": (ny // 2) * 32 + nz * 2 + nc}

    def place(dx, dy):
        nx = (x + sign * dx + 4) % 4
        ny = (y + sign * dy + 4) % 4
        return ((ny // 2) * 4 + nx) * 2 + ny % 2

    def in_group(g, c):
        low = (y_lo + g // 4 + y_hi) % 2
        return {"layer": low * 4 + g % 4, "head": (g // 4) * 32 + z * 2 + c}

    def chip(p):
        return {"layer": (p % 2) * 4 + (p // 2) % 4, "head": (p // 8) * 32 + z * 2 + core}

    partner = device(flip=True)
    sent_to = pick(group, MIRROR)
    got_from = pick(group, MIRRORED)

    barrier = pltpu.get_barrier_semaphore()
    greeted = [device(dx, dy) for dx, dy in OFFSETS]
    greeted += [device(dz=d) for d in (3, -3, 2, -2, 1, -1)]
    greeted += [partner, in_group(sent_to, other), in_group(got_from, other)]
    for d in greeted:
        pl.semaphore_signal(barrier, inc=1, device_id=d, device_id_type=MESH)

    def ready(layer):
        pltpu.make_async_copy(qk_ref.at[layer], qk_ref.at[layer], sin.at[layer]).wait()
        if layer == 0:
            loads[2].wait()
            w = slot_weights(slot_ref, hw_ref)
            w_ref[...] = jnp.broadcast_to(w, (2, TILE))

    forward(w_ref, qk_ref, ready, sc_ref, p_ref, rb_ref, rr_ref, x_ref, e_ref)
    loads[5].wait()
    pl.semaphore_wait(barrier, len(greeted))

    def copy(src, dst, ssem, rsem, dev):
        return pltpu.make_async_remote_copy(
            src_ref=src, dst_ref=dst, send_sem=ssem, recv_sem=rsem, device_id=dev, device_id_type=MESH
        )

    def arrived(ref, rsem):
        copy(ref, ref, s0, rsem, partner).wait_recv()

    def left(ref, ssem):
        copy(ref, ref, ssem, r1, partner).wait_send()

    tile = target_ref.at[:, pl.ds(pl.multiple_of(x * TILE, TILE), TILE)]
    for d, slot in ((1, 1), (-1, 3), (2, 0), (-2, 4), (-3, 5)):
        copy(tile, tn_ref.at[slot], st.at[0], rt.at[0], device(dz=d)).start()
    tn_ref[2] = target_ref[:, pl.ds(pl.multiple_of(x * TILE, TILE), TILE)]

    order = OFFSETS + [(0, 0)]
    copy(e_ref.at[other], a_ref.at[pl.ds(16 * ROWS, 8)], s0, r0.at[0], partner).start()
    for i, (dx, dy) in enumerate(order):
        copy(x_ref.at[other, place(-dx, -dy)], a_ref.at[pl.ds(i * ROWS, ROWS)], s0, r0.at[1 + i // 4], partner).start()

    arrived(a_ref.at[pl.ds(16 * ROWS, 8)], r0.at[0])
    ey_ref[...] = e_ref[core] + a_ref[16 * ROWS : 16 * ROWS + 8, :]
    owner = mine == core * 14
    owner_of_diagonal = {"layer": core * 3, "head": core * 33 + z * 2}

    @pl.when(jnp.logical_not(owner))
    def _():
        copy(ey_ref, eb_ref.at[mine], es.at[0], er.at[0], owner_of_diagonal).start()

    for i, (dx, dy) in enumerate(order):
        if i % 4 == 0:
            arrived(a_ref.at[pl.ds(i * ROWS, 4 * ROWS)], r0.at[1 + i // 4])
        summed = x_ref[core, place(dx, dy)] + a_ref[i * ROWS : (i + 1) * ROWS, :]
        if i < 15:
            y_ref[i] = summed
            copy(y_ref.at[i], b_ref.at[i], s1, r1, device(dx, dy)).start()
        else:
            total = summed

    arrived(t_ref.at[pl.ds(0, 5)], rt.at[0])
    pl.semaphore_signal(relay, inc=1, device_id=device(dz=-5), device_id_type=MESH)
    copy(tn_ref.at[pl.ds(0, 5)], t_ref.at[pl.ds(0, 5)], st.at[0], rt.at[1], device(dz=5)).start()
    copy(tn_ref, t_ref.at[pl.ds(10, 6)], st.at[0], rt.at[1], device(dz=-5)).start()

    arrived(b_ref, r1)
    for i in range(15):
        total = total + b_ref[i]
    z_ref[0] = total
    near = (1, -1, 2, -2)
    for i, d in enumerate(near):
        copy(z_ref.at[0], zn_ref.at[i], sz.at[0], rz.at[0], device(dz=d)).start()
    pl.semaphore_wait(relay, 1)
    copy(z_ref.at[0], zn_ref.at[4], sz.at[0], rz.at[2], device(dz=8)).start()

    @pl.when(owner)
    def _():
        eb_ref[mine] = ey_ref[...]
        arrived(eb_ref.at[pl.ds(0, 15)], er.at[0])
        acc = eb_ref[0]
        for i in range(1, 16):
            acc = acc + eb_ref[i]
        ez_ref[0] = acc
        for i, d in enumerate(near):
            copy(ez_ref.at[0], en_ref.at[i], es.at[1], er.at[1], device(dz=d)).start()
        copy(ez_ref.at[0], en_ref.at[4], es.at[1], er.at[3], device(dz=8)).start()

    arrived(zn_ref.at[pl.ds(0, 4)], rz.at[0])
    for i in range(4):
        total = total + zn_ref[i]
    z_ref[1] = total
    for i, d in enumerate((5, -5)):
        copy(z_ref.at[1], zf_ref.at[i], sz.at[1], rz.at[1], device(dz=d)).start()

    @pl.when(owner)
    def _():
        arrived(en_ref.at[pl.ds(0, 4)], er.at[1])
        acc = ez_ref[0]
        for i in range(4):
            acc = acc + en_ref[i]
        ez_ref[1] = acc
        for i, d in enumerate((5, -5)):
            copy(ez_ref.at[1], ef_ref.at[i], es.at[2], er.at[2], device(dz=d)).start()

    arrived(t_ref.at[pl.ds(0, 11)], rt.at[1])
    for slot in range(16):
        to_ref[(z + sign * (slot - 7) + 16) % 16] = tn_ref[slot - 5] if 5 <= slot < 10 else t_ref[slot]
    keep = pick(group, KEEP)
    kept = to_ref.at[pl.ds(keep * 8, 8)]
    given = to_ref.at[pl.ds((1 - keep) * 8, 8)]
    copy(kept, ta_ref.at[core], st.at[1], rt.at[2], partner).start()
    copy(given, tb_ref.at[core], st.at[2], rt.at[3], in_group(sent_to, core)).start()
    copy(given, tb_ref.at[core], st.at[2], rt.at[3], in_group(sent_to, other)).start()
    ta_ref[core] = to_ref[pl.ds(keep * 8, 8)]
    for layer in range(2):
        qt_ref[layer] = qk_ref[layer, 0].astype(F32).T.astype(BF16)

    arrived(ta_ref.at[other], rt.at[2])
    arrived(tb_ref, rt.at[3])

    def joined(ref):
        return jnp.concatenate([ref[t % 2, t // 2] for t in range(16)], axis=0).astype(F32)

    row = lax.broadcasted_iota(jnp.int32, (TILE, TILE), 0)
    col = lax.broadcasted_iota(jnp.int32, (TILE, TILE), 1)
    first, second = joined(ta_ref), joined(tb_ref)
    first_t, second_t = first.T, second.T
    folded = jnp.where(row < col, first + first_t, second + second_t)
    on_diagonal = jnp.broadcast_to(group % 7, (TILE, TILE)) == 0
    tt_ref[...] = jnp.where(on_diagonal, folded, first + second_t)
    own = jnp.sum(jnp.where(row == col, first, 0.0), axis=0, keepdims=True)
    targets = tt_ref[pl.ds(pl.multiple_of((y_lo * 2 + core) * ROWS, ROWS), ROWS), :]

    arrived(zf_ref, rz.at[1])
    arrived(zn_ref.at[4], rz.at[2])
    total = total + zf_ref[0] + zf_ref[1] + zn_ref[4]
    piece_ref[...] = 2.0 * jax.nn.sigmoid(total) - targets
    for p in range(16):

        @pl.when(mine != p)
        def _(p=p):
            copy(piece_ref, o_ref.at[core, mine], s3, r3.at[mine // 4], chip(p)).start()

    keep_own = pltpu.make_async_copy(piece_ref, o_ref.at[core, mine], r3.at[mine // 4])
    keep_own.start()

    @pl.when(owner)
    def _():
        arrived(ef_ref, er.at[2])
        arrived(en_ref.at[4], er.at[3])
        acc = ez_ref[1] + ef_ref[0] + ef_ref[1] + en_ref[4]
        ep_ref[...] = 2.0 * jax.nn.sigmoid(acc) - 2.0 * own
        for dx, dy in OFFSETS:
            copy(ep_ref, eo_ref.at[core], es.at[3], er.at[4], device(dx, dy)).start()
        copy(ep_ref, eo_ref.at[core], es.at[4], er.at[5], partner).start()
        eo_ref[core] = ep_ref[...]

    for g in range(4):
        pieces = o_ref.at[core, pl.ds(4 * g, 4)]
        arrived(pieces, r3.at[g])
        copy(pieces, pieces, s4, r4, partner).start()

    @pl.when(jnp.logical_not(owner))
    def _():
        arrived(eo_ref.at[core], er.at[4])
        copy(eo_ref.at[core], eo_ref.at[core], es.at[4], er.at[5], partner).start()

    arrived(o_ref.at[other], r4)
    arrived(eo_ref.at[other], er.at[5])
    unpack(o_ref, eo_ref, s_ref)

    left(a_ref, s0)
    left(b_ref, s1)
    left(zn_ref, sz.at[0])
    left(zf_ref, sz.at[1])
    left(t_ref, st.at[0])
    left(ta_ref.at[core], st.at[1])
    left(tb_ref, st.at[2])
    left(b_ref, s3)
    left(o_ref.at[core], s4)
    left(ep_ref, es.at[4])

    @pl.when(owner)
    def _():
        left(en_ref, es.at[1])
        left(ef_ref, es.at[2])
        left(eb_ref.at[pl.ds(0, 15)], es.at[3])

    @pl.when(jnp.logical_not(owner))
    def _():
        left(ey_ref, es.at[0])


def back_kernel(w_ref, qt_ref, qk_ref, p_ref, s_ref, rb_ref, rr_ref, qg_hbm, kg_hbm, wg_hbm, d_ref, ds_ref, qg_ref, kg_ref, wg_ref, sems):
    scale = DH ** (-0.5)
    chunk = 32
    zero = jnp.zeros((8, L), F32)

    def gather(i, carry):
        rows = pl.ds(pl.multiple_of(i * chunk, chunk), chunk)
        s = s_ref[rows, :]
        out = []
        for layer in range(2):
            wide = jnp.concatenate([rb_ref[layer, rows, :]] * 4, axis=1)
            prod = s * wide
            acc = carry[layer]
            for t in range(chunk // 8):
                acc = acc + prod[t * 8 : (t + 1) * 8, :]
            out.append(acc)
        return tuple(out)

    sums = lax.fori_loop(0, L // chunk, gather, (zero, zero), unroll=2)
    grads = []
    stores = []
    h_rows = []
    for layer in range(2):
        h_row = jnp.sum(sums[layer], axis=0, keepdims=True)
        quad = jnp.sum(h_row * rr_ref[layer : layer + 1, :], axis=1, keepdims=True)
        h_scaled = h_row * (1.0 / TOTAL)
        d_row = quad * (1.0 / (TOTAL * TOTAL)) - h_scaled
        for t in range(4):
            wide = jnp.broadcast_to(d_row[:, t * TILE : (t + 1) * TILE], (TILE, TILE))
            d_ref[layer, t * TILE : (t + 1) * TILE, :] = wide.T
        h_rows.append(h_scaled)
        grads.append(-quad * (0.5 / TOTAL))

    def map_rows(layer, i, acc):
        rows = slice(i * chunk, (i + 1) * chunk)
        s = s_ref[rows, :]
        probs = p_ref[layer, rows, :]
        wide = jnp.concatenate([d_ref[layer, rows, :]] * 4, axis=1)
        dprobs = s + wide - h_rows[layer]
        prod = probs * s
        for t in range(chunk // 8):
            acc = acc + prod[t * 8 : (t + 1) * 8, :]
        inner = jnp.sum(probs * dprobs, axis=1, keepdims=True)
        ds_ref[layer, rows, :] = (probs * (dprobs - inner)).astype(BF16)
        return acc

    def query_rows(layer, i, count):
        rows = slice(i * count, (i + 1) * count)
        qg = jnp.dot(ds_ref[layer, rows, :], qk_ref[layer, 1], preferred_element_type=F32)
        qg_ref[layer, rows, :] = (qg * (w_ref[layer : layer + 1, :] * scale)).astype(BF16)

    def key_rows(layer, i, count):
        rows = slice(i * count, (i + 1) * count)
        kg = jnp.dot(qt_ref[layer], ds_ref[layer, :, rows], preferred_element_type=F32)
        kg_ref[layer, rows, :] = (kg.T * (w_ref[layer : layer + 1, :] * scale)).astype(BF16)

    def store(src, dst, index):
        stores.append(pltpu.make_async_copy(src, dst, sems.at[index]))
        stores[-1].start()

    acc = zero
    for i in range(16):
        acc = map_rows(0, i, acc)
    grads[0] = grads[0] + jnp.sum(jnp.sum(acc, axis=0, keepdims=True), axis=1, keepdims=True)
    acc = zero
    for i in range(16):
        acc = map_rows(1, i, acc)
        if i % 8 == 3:
            query_rows(0, i // 8, 256)
        if i % 8 == 7:
            key_rows(0, i // 8, 256)
    grads[1] = grads[1] + jnp.sum(jnp.sum(acc, axis=0, keepdims=True), axis=1, keepdims=True)
    lane = lax.broadcasted_iota(jnp.int32, (1, 2), 1)
    wg_ref[...] = jnp.where(lane == 0, grads[0], grads[1])
    store(wg_ref, wg_hbm, 5)
    store(qg_ref.at[0], qg_hbm.at[0], 0)
    store(kg_ref.at[0], kg_hbm.at[0], 1)
    for i in range(2):
        key_rows(1, i, 256)
    store(kg_ref.at[1], kg_hbm.at[1], 2)
    for i in range(2):
        query_rows(1, i, 256)
        rows = pl.ds(i * 256, 256)
        store(qg_ref.at[1, rows], qg_hbm.at[1, rows], 3 + i)
    for c in stores:
        c.wait()


def vmem():
    return pl.BlockSpec(memory_space=pltpu.VMEM)


def smem():
    return pl.BlockSpec(memory_space=pltpu.SMEM)


def hbm():
    return pl.BlockSpec(memory_space=pltpu.HBM)


def on_device(queries, keys, head_weight, slot_head, target):
    q = queries.reshape(2, L, DH)
    k = keys.reshape(2, L, DH)
    dma = pltpu.SemaphoreType.DMA
    probs, s_map, rb, rr, w, qk, q_turned = pl.pallas_call(
        exchange_kernel,
        out_shape=(
            pltpu.VMEM((2, L, L), F32),
            pltpu.VMEM((L, L), F32),
            pltpu.VMEM((2, L, TILE), F32),
            pltpu.VMEM((2, L), F32),
            pltpu.VMEM((2, TILE), F32),
            pltpu.VMEM((2, 2, L, DH), BF16),
            pltpu.VMEM((2, DH, L), BF16),
        ),
        in_specs=[smem()] + [hbm()] * 4,
        out_specs=(vmem(),) * 7,
        scratch_shapes=[
            pltpu.VMEM((2, 40), F32),
            pltpu.VMEM((8, L), jnp.int32),
            pltpu.VMEM((2, L, L), F32),
            pltpu.VMEM((2, 16, ROWS, TILE), F32),
            pltpu.VMEM((16 * ROWS + 8, TILE), F32),
            pltpu.VMEM((15, ROWS, TILE), F32),
            pltpu.VMEM((15, ROWS, TILE), F32),
            pltpu.VMEM((3, ROWS, TILE), F32),
            pltpu.VMEM((5, ROWS, TILE), F32),
            pltpu.VMEM((2, ROWS, TILE), F32),
            pltpu.VMEM((6, 8, TILE), jnp.int32),
            pltpu.VMEM((16, 8, TILE), jnp.int32),
            pltpu.VMEM((16, 8, TILE), jnp.int32),
            pltpu.VMEM((2, 8, 8, TILE), jnp.int32),
            pltpu.VMEM((2, 8, 8, TILE), jnp.int32),
            pltpu.VMEM((TILE, TILE), F32),
            pltpu.VMEM((ROWS, TILE), F32),
            pltpu.VMEM((2, 16, ROWS, TILE), F32),
            pltpu.VMEM((2, 8, TILE), F32),
            pltpu.VMEM((8, TILE), F32),
            pltpu.VMEM((16, 8, TILE), F32),
            pltpu.VMEM((3, 8, TILE), F32),
            pltpu.VMEM((5, 8, TILE), F32),
            pltpu.VMEM((2, 8, TILE), F32),
            pltpu.VMEM((8, TILE), F32),
            pltpu.VMEM((2, 8, TILE), F32),
            dma((4,)), dma, dma((5,)), dma, dma, dma((2,)), dma((3,)), dma((3,)), dma((4,)),
            dma, dma((4,)), dma, dma, dma((5,)), dma((6,)), pltpu.SemaphoreType.REGULAR,
        ],
        compiler_params=pltpu.CompilerParams(collective_id=0, has_side_effects=True, vmem_limit_bytes=16 << 20),
    )(slot_head, *[pltpu.with_memory_space_constraint(v, pltpu.HBM) for v in (head_weight, target, q, k)])
    qg, kg, wg = pl.pallas_call(
        back_kernel,
        out_shape=(
            jax.ShapeDtypeStruct((2, L, DH), BF16),
            jax.ShapeDtypeStruct((2, L, DH), BF16),
            jax.ShapeDtypeStruct((1, 2), F32),
        ),
        in_specs=[vmem()] * 7,
        out_specs=(hbm(), hbm(), hbm()),
        scratch_shapes=[
            pltpu.VMEM((2, L, TILE), F32),
            pltpu.VMEM((2, L, L), BF16),
            pltpu.VMEM((2, L, DH), BF16),
            pltpu.VMEM((2, L, DH), BF16),
            pltpu.VMEM((1, 2), F32),
            pltpu.SemaphoreType.DMA((6,)),
        ],
        compiler_params=pltpu.CompilerParams(vmem_limit_bytes=16 << 20),
    )(w, q_turned, qk, probs, s_map, rb, rr)
    return (qg.reshape(2, 1, L, DH), kg.reshape(2, 1, L, DH), wg.reshape(2, 1))


def solution(mesh):
    placed = (
        P("layer", "head", None, None),
        P("layer", "head", None, None),
        P("layer", None),
        P("head"),
        P("head", None),
    )
    return jax.shard_map(
        on_device,
        mesh=mesh,
        in_specs=placed,
        out_specs=(P("layer", "head", None, None), P("layer", "head", None, None), P("layer", "head")),
        check_vma=False,
    )
```

```python
import jax
import jax.numpy as jnp
from jax import lax
from jax.experimental import pallas as pl
from jax.experimental.pallas import tpu as pltpu
from jax.sharding import PartitionSpec as P

MESH = pl.DeviceIdType.MESH
F32 = jnp.float32
BF16 = jnp.bfloat16
L = 512
DH = 128
TILE = 128
TOTAL = 2.0 * L
OFF = {1: (0, 1), 2: (0, 2), 3: (1, 3), 4: (3, 0), 5: (2, 1), 6: (3, 2)}
DIAG = {0: (0, 1), 7: (3, 2)}
KEEP = (0, 0, 0, 1, 1, 0, 1, 1)
MIRROR = (1, 0, 5, 4, 2, 3, 7, 6)
MIRRORED = (1, 0, 4, 5, 3, 2, 7, 6)
ROWS = 32
OFFSETS = sorted(
    ((dx, dy) for dx in range(4) for dy in range(4) if dx or dy),
    key=lambda o: -(min(o[0], 4 - o[0]) + min(o[1], 4 - o[1])),
)


def pick(index, table):
    value = jnp.int32(table[0])
    for k in range(1, len(table)):
        value = jnp.where(index == k, jnp.int32(table[k]), value)
    return value


def slot_weights(slot_ref, hw_ref):
    hw = hw_ref[...]
    lane = lax.broadcasted_iota(jnp.int32, hw.shape, 1)
    return jnp.sum(jnp.where(lane == slot_ref[0], hw, 0.0), axis=1, keepdims=True)


def forward(w, qk_ref, ready, sc_ref, p_ref, rb_ref, rr_ref, x_ref, e_ref):
    scale = DH ** (-0.5)
    chunk = 32
    sums = []
    for layer in range(2):
        ready(layer)
        sc_ref[layer] = lax.dot_general(
            qk_ref[layer, 0], qk_ref[layer, 1], (((1,), (1,)), ((), ())), preferred_element_type=F32
        )
    for layer in range(2):

        def body(i, csum, layer=layer):
            rows = pl.ds(pl.multiple_of(i * chunk, chunk), chunk)
            scores = sc_ref[layer, rows, :]
            highest = jnp.max(scores, axis=1, keepdims=True)
            expo = jnp.exp((scores - highest) * scale)
            probs = expo * (1.0 / jnp.sum(expo, axis=1, keepdims=True))
            p_ref[layer, rows, :] = probs
            for t in range(chunk // 8):
                csum = csum + probs[t * 8 : (t + 1) * 8, :]
            return csum

        csum = lax.fori_loop(0, L // chunk, body, jnp.zeros((8, L), F32), unroll=16)
        rowsum = 1.0 + jnp.sum(csum, axis=0, keepdims=True)
        rr_ref[layer : layer + 1, :] = rowsum
        for t in range(4):
            wide = jnp.broadcast_to(rowsum[:, t * TILE : (t + 1) * TILE], (TILE, TILE))
            rb_ref[layer, t * TILE : (t + 1) * TILE, :] = wide.T
        sums.append(rowsum * (w[layer : layer + 1, 0:1] / TOTAL))

    def cut(t):
        return slice(t * TILE, (t + 1) * TILE)

    def half(a, b):
        return w[0:1, :] * p_ref[0, cut(a), cut(b)] + w[1:2, :] * p_ref[1, cut(a), cut(b)]

    def block(a, b):
        outer = rb_ref[0, cut(a), :] * sums[0][:, cut(b)] + rb_ref[1, cut(a), :] * sums[1][:, cut(b)]
        return half(a, b) + half(b, a).T - outer

    row = lax.broadcasted_iota(jnp.int32, (TILE, TILE), 0)
    col = lax.broadcasted_iota(jnp.int32, (TILE, TILE), 1)
    for g in range(8):
        if g in OFF:
            full = block(*OFF[g])
        else:
            upper = block(DIAG[g][0], DIAG[g][0])
            full = jnp.where(row < col, upper, block(DIAG[g][1], DIAG[g][1]))
            extra = jnp.sum(jnp.where(row == col, upper, 0.0), axis=0, keepdims=True)
            e_ref[g // 7] = jnp.broadcast_to(extra, (8, TILE))
        for part in range(4):
            x_ref[part % 2, 2 * g + part // 2] = full[part * ROWS : (part + 1) * ROWS, :]


def unpack(o_ref, eo_ref, rb_ref, s_ref, h_ref):
    row = lax.broadcasted_iota(jnp.int32, (TILE, TILE), 0)
    col = lax.broadcasted_iota(jnp.int32, (TILE, TILE), 1)

    def cut(t):
        return slice(t * TILE, (t + 1) * TILE)

    sums = [[jnp.zeros((8, TILE), F32)] * 4 for _ in range(2)]

    def put(a, b, value):
        s_ref[cut(a), cut(b)] = value
        for layer in range(2):
            weighted = rb_ref[layer, cut(a), :] * value
            for t in range(TILE // 8):
                sums[layer][b] = sums[layer][b] + weighted[t * 8 : (t + 1) * 8, :]

    for g in range(8):
        full = jnp.concatenate([o_ref[part % 2, 2 * g + part // 2] for part in range(4)], axis=0)
        if g in OFF:
            a, b = OFF[g]
            put(a, b, full)
            put(b, a, full.T)
        else:
            a, b = DIAG[g]
            turned = full.T
            diagonal = eo_ref[g // 7, 0:1, :]
            upper = jnp.where(row < col, full, jnp.where(row == col, diagonal, turned))
            put(a, a, upper)
            put(b, b, jnp.where(row < col, turned, full))
    for layer in range(2):
        for t in range(4):
            h_ref[layer, :, cut(t)] = sums[layer][t]


def exchange_kernel(
    slot_ref, hw_hbm, target_hbm, q_hbm, k_hbm,
    p_ref, s_ref, h_ref, rr_ref, w_ref, qk_ref, qt_ref, rb_ref,
    hw_ref, target_ref, sc_ref, x_ref, a_ref, y_ref, b_ref, z_ref, zn_ref, zf_ref,
    tn_ref, t_ref, to_ref, ta_ref, tb_ref, tt_ref, piece_ref, o_ref,
    e_ref, ey_ref, eb_ref, ez_ref, en_ref, ef_ref, ep_ref, eo_ref,
    sin, s0, r0, s1, r1, sz, rz, st, rt, s3, r3, s4, r4, es, er, relay,
):
    loads = [
        pltpu.make_async_copy(q_hbm.at[0], qk_ref.at[0, 0], sin.at[0]),
        pltpu.make_async_copy(k_hbm.at[0], qk_ref.at[0, 1], sin.at[0]),
        pltpu.make_async_copy(hw_hbm, hw_ref, sin.at[2]),
        pltpu.make_async_copy(q_hbm.at[1], qk_ref.at[1, 0], sin.at[1]),
        pltpu.make_async_copy(k_hbm.at[1], qk_ref.at[1, 1], sin.at[1]),
        pltpu.make_async_copy(target_hbm, target_ref, sin.at[3]),
    ]
    for c in loads:
        c.start()
    layer_pos = lax.axis_index("layer")
    head_pos = lax.axis_index("head")
    x = layer_pos % 4
    y_lo = layer_pos // 4
    core = head_pos % 2
    z = (head_pos // 2) % 16
    y_hi = head_pos // 32
    y = y_hi * 2 + y_lo
    group = y_hi * 4 + x
    other = 1 - core
    mine = group * 2 + y_lo
    sign = 1 - 2 * core

    def device(dx=0, dy=0, dz=0, flip=False):
        nx = (x + sign * dx + 4) % 4
        ny = (y + sign * dy + 4) % 4
        nz = (z + sign * dz + 16) % 16
        nc = other if flip else core
        return {"layer": (ny % 2) * 4 + nx, "head": (ny // 2) * 32 + nz * 2 + nc}

    def place(dx, dy):
        nx = (x + sign * dx + 4) % 4
        ny = (y + sign * dy + 4) % 4
        return ((ny // 2) * 4 + nx) * 2 + ny % 2

    def in_group(g, c):
        low = (y_lo + g // 4 + y_hi) % 2
        return {"layer": low * 4 + g % 4, "head": (g // 4) * 32 + z * 2 + c}

    def chip(p):
        return {"layer": (p % 2) * 4 + (p // 2) % 4, "head": (p // 8) * 32 + z * 2 + core}

    partner = device(flip=True)
    sent_to = pick(group, MIRROR)
    got_from = pick(group, MIRRORED)

    barrier = pltpu.get_barrier_semaphore()
    greeted = [device(dx, dy) for dx, dy in OFFSETS]
    greeted += [device(dz=d) for d in (3, -3, 2, -2, 1, -1)]
    greeted += [partner, in_group(sent_to, other), in_group(got_from, other)]
    for d in greeted:
        pl.semaphore_signal(barrier, inc=1, device_id=d, device_id_type=MESH)

    def ready(layer):
        pltpu.make_async_copy(qk_ref.at[layer], qk_ref.at[layer], sin.at[layer]).wait()
        if layer == 0:
            loads[2].wait()
            w = slot_weights(slot_ref, hw_ref)
            w_ref[...] = jnp.broadcast_to(w, (2, TILE))

    forward(w_ref, qk_ref, ready, sc_ref, p_ref, rb_ref, rr_ref, x_ref, e_ref)
    loads[5].wait()
    pl.semaphore_wait(barrier, len(greeted))

    def copy(src, dst, ssem, rsem, dev):
        return pltpu.make_async_remote_copy(
            src_ref=src, dst_ref=dst, send_sem=ssem, recv_sem=rsem, device_id=dev, device_id_type=MESH
        )

    def arrived(ref, rsem):
        copy(ref, ref, s0, rsem, partner).wait_recv()

    def left(ref, ssem):
        copy(ref, ref, ssem, r1, partner).wait_send()

    tile = target_ref.at[:, pl.ds(pl.multiple_of(x * TILE, TILE), TILE)]
    for d, slot in ((1, 1), (-1, 3), (2, 0), (-2, 4)):
        copy(tile, tn_ref.at[slot], st.at[0], rt.at[0], device(dz=d)).start()
    copy(tile, tn_ref.at[5], st.at[0], rt.at[4], device(dz=-3)).start()
    tn_ref[2] = target_ref[:, pl.ds(pl.multiple_of(x * TILE, TILE), TILE)]

    order = OFFSETS + [(0, 0)]
    copy(e_ref.at[other], a_ref.at[pl.ds(16 * ROWS, 8)], s0, r0.at[0], partner).start()
    for i, (dx, dy) in enumerate(order):
        copy(x_ref.at[other, place(-dx, -dy)], a_ref.at[pl.ds(i * ROWS, ROWS)], s0, r0.at[1 + i // 4], partner).start()

    arrived(a_ref.at[pl.ds(16 * ROWS, 8)], r0.at[0])
    ey_ref[...] = e_ref[core] + a_ref[16 * ROWS : 16 * ROWS + 8, :]
    owner = mine == core * 14
    owner_of_diagonal = {"layer": core * 3, "head": core * 33 + z * 2}

    @pl.when(jnp.logical_not(owner))
    def _():
        copy(ey_ref, eb_ref.at[mine], es.at[0], er.at[0], owner_of_diagonal).start()

    for i, (dx, dy) in enumerate(order):
        if i % 4 == 0:
            arrived(a_ref.at[pl.ds(i * ROWS, 4 * ROWS)], r0.at[1 + i // 4])
        summed = x_ref[core, place(dx, dy)] + a_ref[i * ROWS : (i + 1) * ROWS, :]
        if i < 15:
            y_ref[i] = summed
            copy(y_ref.at[i], b_ref.at[i], s1, r1, device(dx, dy)).start()
        else:
            total = summed

    arrived(t_ref.at[pl.ds(0, 4)], rt.at[0])
    pl.semaphore_signal(relay, inc=1, device_id=device(dz=-5), device_id_type=MESH)
    copy(tn_ref.at[pl.ds(0, 5)], t_ref.at[pl.ds(0, 5)], st.at[0], rt.at[1], device(dz=5)).start()
    arrived(tn_ref.at[5], rt.at[4])
    copy(tn_ref, t_ref.at[pl.ds(10, 6)], st.at[0], rt.at[1], device(dz=-5)).start()

    arrived(b_ref, r1)
    for i in range(15):
        total = total + b_ref[i]
    z_ref[0] = total
    near = (1, -1, 2, -2)
    for i, d in enumerate(near):
        copy(z_ref.at[0], zn_ref.at[i], sz.at[0], rz.at[0], device(dz=d)).start()
    @pl.when(owner)
    def _():
        eb_ref[mine] = ey_ref[...]
        arrived(eb_ref.at[pl.ds(0, 15)], er.at[0])
        acc = eb_ref[0]
        for i in range(1, 16):
            acc = acc + eb_ref[i]
        ez_ref[0] = acc
        for i, d in enumerate(near):
            copy(ez_ref.at[0], en_ref.at[i], es.at[1], er.at[1], device(dz=d)).start()

    pl.semaphore_wait(relay, 1)
    copy(z_ref.at[0], zn_ref.at[4], sz.at[0], rz.at[2], device(dz=8)).start()

    @pl.when(owner)
    def _():
        copy(ez_ref.at[0], en_ref.at[4], es.at[1], er.at[3], device(dz=8)).start()

    arrived(zn_ref.at[pl.ds(0, 4)], rz.at[0])
    for i in range(4):
        total = total + zn_ref[i]
    z_ref[1] = total
    for i, d in enumerate((5, -5)):
        copy(z_ref.at[1], zf_ref.at[i], sz.at[1], rz.at[1], device(dz=d)).start()

    @pl.when(owner)
    def _():
        arrived(en_ref.at[pl.ds(0, 4)], er.at[1])
        acc = ez_ref[0]
        for i in range(4):
            acc = acc + en_ref[i]
        ez_ref[1] = acc
        for i, d in enumerate((5, -5)):
            copy(ez_ref.at[1], ef_ref.at[i], es.at[2], er.at[2], device(dz=d)).start()

    arrived(t_ref.at[pl.ds(0, 11)], rt.at[1])
    for slot in range(16):
        to_ref[(z + sign * (slot - 7) + 16) % 16] = tn_ref[slot - 5] if 5 <= slot < 10 else t_ref[slot]
    keep = pick(group, KEEP)
    kept = to_ref.at[pl.ds(keep * 8, 8)]
    given = to_ref.at[pl.ds((1 - keep) * 8, 8)]
    copy(kept, ta_ref.at[core], st.at[1], rt.at[2], partner).start()
    copy(given, tb_ref.at[core], st.at[2], rt.at[3], in_group(sent_to, core)).start()
    copy(given, tb_ref.at[core], st.at[2], rt.at[3], in_group(sent_to, other)).start()
    ta_ref[core] = to_ref[pl.ds(keep * 8, 8)]
    for layer in range(2):
        qt_ref[layer] = qk_ref[layer, 0].astype(F32).T.astype(BF16)

    arrived(ta_ref.at[other], rt.at[2])
    arrived(tb_ref, rt.at[3])

    def joined(ref):
        return jnp.concatenate([ref[t % 2, t // 2] for t in range(16)], axis=0).astype(F32)

    row = lax.broadcasted_iota(jnp.int32, (TILE, TILE), 0)
    col = lax.broadcasted_iota(jnp.int32, (TILE, TILE), 1)
    first, second = joined(ta_ref), joined(tb_ref)
    first_t, second_t = first.T, second.T
    folded = jnp.where(row < col, first + first_t, second + second_t)
    on_diagonal = jnp.broadcast_to(group % 7, (TILE, TILE)) == 0
    tt_ref[...] = jnp.where(on_diagonal, folded, first + second_t)
    own = jnp.sum(jnp.where(row == col, first, 0.0), axis=0, keepdims=True)
    targets = tt_ref[pl.ds(pl.multiple_of((y_lo * 2 + core) * ROWS, ROWS), ROWS), :]

    arrived(zf_ref, rz.at[1])
    arrived(zn_ref.at[4], rz.at[2])
    total = total + zf_ref[0] + zf_ref[1] + zn_ref[4]
    piece_ref[...] = 2.0 * jax.nn.sigmoid(total) - targets
    for p in range(16):

        @pl.when(mine != p)
        def _(p=p):
            copy(piece_ref, o_ref.at[core, mine], s3, r3.at[mine // 4], chip(p)).start()

    keep_own = pltpu.make_async_copy(piece_ref, o_ref.at[core, mine], r3.at[mine // 4])
    keep_own.start()

    @pl.when(owner)
    def _():
        arrived(ef_ref, er.at[2])
        arrived(en_ref.at[4], er.at[3])
        acc = ez_ref[1] + ef_ref[0] + ef_ref[1] + en_ref[4]
        ep_ref[...] = 2.0 * jax.nn.sigmoid(acc) - 2.0 * own
        for dx, dy in OFFSETS:
            copy(ep_ref, eo_ref.at[core], es.at[3], er.at[4], device(dx, dy)).start()
        copy(ep_ref, eo_ref.at[core], es.at[4], er.at[5], partner).start()
        eo_ref[core] = ep_ref[...]

    for g in range(4):
        pieces = o_ref.at[core, pl.ds(4 * g, 4)]
        arrived(pieces, r3.at[g])
        copy(pieces, pieces, s4, r4, partner).start()

    @pl.when(jnp.logical_not(owner))
    def _():
        arrived(eo_ref.at[core], er.at[4])
        copy(eo_ref.at[core], eo_ref.at[core], es.at[4], er.at[5], partner).start()

    arrived(o_ref.at[other], r4)
    arrived(eo_ref.at[other], er.at[5])
    unpack(o_ref, eo_ref, rb_ref, s_ref, h_ref)

    left(a_ref, s0)
    left(b_ref, s1)
    left(zn_ref, sz.at[0])
    left(zf_ref, sz.at[1])
    left(t_ref, st.at[0])
    left(ta_ref.at[core], st.at[1])
    left(tb_ref, st.at[2])
    left(b_ref, s3)
    left(o_ref.at[core], s4)
    left(ep_ref, es.at[4])

    @pl.when(owner)
    def _():
        left(en_ref, es.at[1])
        left(ef_ref, es.at[2])
        left(eb_ref.at[pl.ds(0, 15)], es.at[3])

    @pl.when(jnp.logical_not(owner))
    def _():
        left(ey_ref, es.at[0])


def back_kernel(w_ref, qt_ref, qk_ref, p_ref, s_ref, h_ref, rr_ref, qg_hbm, kg_hbm, wg_hbm, d_ref, ds_ref, qg_ref, kg_ref, wg_ref, sems):
    scale = DH ** (-0.5)
    chunk = 32
    zero = jnp.zeros((8, L), F32)

    grads = []
    stores = []
    h_rows = []
    for layer in range(2):
        h_row = jnp.sum(h_ref[layer], axis=0, keepdims=True)
        quad = jnp.sum(h_row * rr_ref[layer : layer + 1, :], axis=1, keepdims=True)
        h_scaled = h_row * (1.0 / TOTAL)
        d_row = quad * (1.0 / (TOTAL * TOTAL)) - h_scaled
        for t in range(4):
            wide = jnp.broadcast_to(d_row[:, t * TILE : (t + 1) * TILE], (TILE, TILE))
            d_ref[layer, t * TILE : (t + 1) * TILE, :] = wide.T
        h_rows.append(h_scaled)
        grads.append(-quad * (0.5 / TOTAL))

    def map_rows(layer, i, acc):
        rows = slice(i * chunk, (i + 1) * chunk)
        s = s_ref[rows, :]
        probs = p_ref[layer, rows, :]
        wide = jnp.concatenate([d_ref[layer, rows, :]] * 4, axis=1)
        dprobs = s + wide - h_rows[layer]
        prod = probs * s
        for t in range(chunk // 8):
            acc = acc + prod[t * 8 : (t + 1) * 8, :]
        inner = jnp.sum(probs * dprobs, axis=1, keepdims=True)
        ds_ref[layer, rows, :] = (probs * (dprobs - inner)).astype(BF16)
        return acc

    def query_rows(layer, i, count):
        rows = slice(i * count, (i + 1) * count)
        qg = jnp.dot(ds_ref[layer, rows, :], qk_ref[layer, 1], preferred_element_type=F32)
        qg_ref[layer, rows, :] = (qg * (w_ref[layer : layer + 1, :] * scale)).astype(BF16)

    def key_rows(layer, i, count):
        rows = slice(i * count, (i + 1) * count)
        kg = jnp.dot(qt_ref[layer], ds_ref[layer, :, rows], preferred_element_type=F32)
        kg_ref[layer, rows, :] = (kg.T * (w_ref[layer : layer + 1, :] * scale)).astype(BF16)

    def store(src, dst, index):
        stores.append(pltpu.make_async_copy(src, dst, sems.at[index]))
        stores[-1].start()

    acc = zero
    for i in range(16):
        acc = map_rows(0, i, acc)
    grads[0] = grads[0] + jnp.sum(jnp.sum(acc, axis=0, keepdims=True), axis=1, keepdims=True)
    acc = zero
    for i in range(16):
        acc = map_rows(1, i, acc)
        if i % 8 == 3:
            query_rows(0, i // 8, 256)
        if i % 8 == 7:
            key_rows(0, i // 8, 256)
    grads[1] = grads[1] + jnp.sum(jnp.sum(acc, axis=0, keepdims=True), axis=1, keepdims=True)
    lane = lax.broadcasted_iota(jnp.int32, (1, 2), 1)
    wg_ref[...] = jnp.where(lane == 0, grads[0], grads[1])
    store(wg_ref, wg_hbm, 5)
    store(qg_ref.at[0], qg_hbm.at[0], 0)
    store(kg_ref.at[0], kg_hbm.at[0], 1)
    for i in range(2):
        key_rows(1, i, 256)
    store(kg_ref.at[1], kg_hbm.at[1], 2)
    for i in range(2):
        query_rows(1, i, 256)
        rows = pl.ds(i * 256, 256)
        store(qg_ref.at[1, rows], qg_hbm.at[1, rows], 3 + i)
    for c in stores:
        c.wait()


def vmem():
    return pl.BlockSpec(memory_space=pltpu.VMEM)


def smem():
    return pl.BlockSpec(memory_space=pltpu.SMEM)


def hbm():
    return pl.BlockSpec(memory_space=pltpu.HBM)


def on_device(queries, keys, head_weight, slot_head, target):
    q = queries.reshape(2, L, DH)
    k = keys.reshape(2, L, DH)
    dma = pltpu.SemaphoreType.DMA
    probs, s_map, h, rr, w, qk, q_turned = pl.pallas_call(
        exchange_kernel,
        out_shape=(
            pltpu.VMEM((2, L, L), F32),
            pltpu.VMEM((L, L), F32),
            pltpu.VMEM((2, 8, L), F32),
            pltpu.VMEM((2, L), F32),
            pltpu.VMEM((2, TILE), F32),
            pltpu.VMEM((2, 2, L, DH), BF16),
            pltpu.VMEM((2, DH, L), BF16),
        ),
        in_specs=[smem()] + [hbm()] * 4,
        out_specs=(vmem(),) * 7,
        scratch_shapes=[
            pltpu.VMEM((2, L, TILE), F32),
            pltpu.VMEM((2, 40), F32),
            pltpu.VMEM((8, L), jnp.int32),
            pltpu.VMEM((2, L, L), F32),
            pltpu.VMEM((2, 16, ROWS, TILE), F32),
            pltpu.VMEM((16 * ROWS + 8, TILE), F32),
            pltpu.VMEM((15, ROWS, TILE), F32),
            pltpu.VMEM((15, ROWS, TILE), F32),
            pltpu.VMEM((3, ROWS, TILE), F32),
            pltpu.VMEM((5, ROWS, TILE), F32),
            pltpu.VMEM((2, ROWS, TILE), F32),
            pltpu.VMEM((6, 8, TILE), jnp.int32),
            pltpu.VMEM((16, 8, TILE), jnp.int32),
            pltpu.VMEM((16, 8, TILE), jnp.int32),
            pltpu.VMEM((2, 8, 8, TILE), jnp.int32),
            pltpu.VMEM((2, 8, 8, TILE), jnp.int32),
            pltpu.VMEM((TILE, TILE), F32),
            pltpu.VMEM((ROWS, TILE), F32),
            pltpu.VMEM((2, 16, ROWS, TILE), F32),
            pltpu.VMEM((2, 8, TILE), F32),
            pltpu.VMEM((8, TILE), F32),
            pltpu.VMEM((16, 8, TILE), F32),
            pltpu.VMEM((3, 8, TILE), F32),
            pltpu.VMEM((5, 8, TILE), F32),
            pltpu.VMEM((2, 8, TILE), F32),
            pltpu.VMEM((8, TILE), F32),
            pltpu.VMEM((2, 8, TILE), F32),
            dma((4,)), dma, dma((5,)), dma, dma, dma((2,)), dma((3,)), dma((3,)), dma((5,)),
            dma, dma((4,)), dma, dma, dma((5,)), dma((6,)), pltpu.SemaphoreType.REGULAR,
        ],
        compiler_params=pltpu.CompilerParams(collective_id=0, has_side_effects=True, vmem_limit_bytes=16 << 20),
    )(slot_head, *[pltpu.with_memory_space_constraint(v, pltpu.HBM) for v in (head_weight, target, q, k)])
    qg, kg, wg = pl.pallas_call(
        back_kernel,
        out_shape=(
            jax.ShapeDtypeStruct((2, L, DH), BF16),
            jax.ShapeDtypeStruct((2, L, DH), BF16),
            jax.ShapeDtypeStruct((1, 2), F32),
        ),
        in_specs=[vmem()] * 7,
        out_specs=(hbm(), hbm(), hbm()),
        scratch_shapes=[
            pltpu.VMEM((2, L, TILE), F32),
            pltpu.VMEM((2, L, L), BF16),
            pltpu.VMEM((2, L, DH), BF16),
            pltpu.VMEM((2, L, DH), BF16),
            pltpu.VMEM((1, 2), F32),
            pltpu.SemaphoreType.DMA((6,)),
        ],
        compiler_params=pltpu.CompilerParams(vmem_limit_bytes=16 << 20),
    )(w, q_turned, qk, probs, s_map, h, rr)
    return (qg.reshape(2, 1, L, DH), kg.reshape(2, 1, L, DH), wg.reshape(2, 1))


def solution(mesh):
    placed = (
        P("layer", "head", None, None),
        P("layer", "head", None, None),
        P("layer", None),
        P("head"),
        P("head", None),
    )
    return jax.shard_map(
        on_device,
        mesh=mesh,
        in_specs=placed,
        out_specs=(P("layer", "head", None, None), P("layer", "head", None, None), P("layer", "head")),
        check_vma=False,
    )
```

```python
import jax
import jax.numpy as jnp
from jax import lax
from jax.experimental import pallas as pl
from jax.experimental.pallas import tpu as pltpu
from jax.sharding import PartitionSpec as P

MESH = pl.DeviceIdType.MESH
F32 = jnp.float32
BF16 = jnp.bfloat16
L = 512
DH = 128
TILE = 128
TOTAL = 2.0 * L
OFF = {1: (0, 1), 2: (0, 2), 3: (1, 3), 4: (3, 0), 5: (2, 1), 6: (3, 2)}
DIAG = {0: (0, 1), 7: (3, 2)}
KEEP = (0, 0, 0, 1, 1, 0, 1, 1)
MIRROR = (1, 0, 5, 4, 2, 3, 7, 6)
MIRRORED = (1, 0, 4, 5, 3, 2, 7, 6)
ROWS = 32
OFFSETS = sorted(
    ((dx, dy) for dx in range(4) for dy in range(4) if dx or dy),
    key=lambda o: -(min(o[0], 4 - o[0]) + min(o[1], 4 - o[1])),
)


def pick(index, table):
    value = jnp.int32(table[0])
    for k in range(1, len(table)):
        value = jnp.where(index == k, jnp.int32(table[k]), value)
    return value


def slot_weights(slot_ref, hw_ref):
    hw = hw_ref[...]
    lane = lax.broadcasted_iota(jnp.int32, hw.shape, 1)
    return jnp.sum(jnp.where(lane == slot_ref[0], hw, 0.0), axis=1, keepdims=True)


def forward(w, qk_ref, ready, sc_ref, p_ref, rb_ref, rr_ref, x_ref, e_ref):
    scale = DH ** (-0.5)
    chunk = 32
    sums = []
    for layer in range(2):
        ready(layer)
        sc_ref[layer] = lax.dot_general(
            qk_ref[layer, 0], qk_ref[layer, 1], (((1,), (1,)), ((), ())), preferred_element_type=F32
        )
    for layer in range(2):

        def body(i, csum, layer=layer):
            rows = pl.ds(pl.multiple_of(i * chunk, chunk), chunk)
            scores = sc_ref[layer, rows, :]
            highest = jnp.max(scores, axis=1, keepdims=True)
            expo = jnp.exp((scores - highest) * scale)
            probs = expo * (1.0 / jnp.sum(expo, axis=1, keepdims=True))
            p_ref[layer, rows, :] = probs
            for t in range(chunk // 8):
                csum = csum + probs[t * 8 : (t + 1) * 8, :]
            return csum

        csum = lax.fori_loop(0, L // chunk, body, jnp.zeros((8, L), F32), unroll=16)
        rowsum = 1.0 + jnp.sum(csum, axis=0, keepdims=True)
        rr_ref[layer : layer + 1, :] = rowsum
        for t in range(4):
            wide = jnp.broadcast_to(rowsum[:, t * TILE : (t + 1) * TILE], (TILE, TILE))
            rb_ref[layer, t * TILE : (t + 1) * TILE, :] = wide.T
        sums.append(rowsum * (w[layer : layer + 1, 0:1] / TOTAL))

    def cut(t):
        return slice(t * TILE, (t + 1) * TILE)

    def half(a, b):
        return w[0:1, :] * p_ref[0, cut(a), cut(b)] + w[1:2, :] * p_ref[1, cut(a), cut(b)]

    def block(a, b):
        outer = rb_ref[0, cut(a), :] * sums[0][:, cut(b)] + rb_ref[1, cut(a), :] * sums[1][:, cut(b)]
        return half(a, b) + half(b, a).T - outer

    row = lax.broadcasted_iota(jnp.int32, (TILE, TILE), 0)
    col = lax.broadcasted_iota(jnp.int32, (TILE, TILE), 1)
    for g in range(8):
        if g in OFF:
            full = block(*OFF[g])
        else:
            upper = block(DIAG[g][0], DIAG[g][0])
            full = jnp.where(row < col, upper, block(DIAG[g][1], DIAG[g][1]))
            extra = jnp.sum(jnp.where(row == col, upper, 0.0), axis=0, keepdims=True)
            e_ref[g // 7] = jnp.broadcast_to(extra, (8, TILE))
        for part in range(4):
            x_ref[part % 2, 2 * g + part // 2] = full[part * ROWS : (part + 1) * ROWS, :]


def unpack(o_ref, eo_ref, rb_ref, s_ref, h_ref):
    row = lax.broadcasted_iota(jnp.int32, (TILE, TILE), 0)
    col = lax.broadcasted_iota(jnp.int32, (TILE, TILE), 1)

    def cut(t):
        return slice(t * TILE, (t + 1) * TILE)

    sums = [[jnp.zeros((8, TILE), F32)] * 4 for _ in range(2)]

    def put(a, b, value):
        s_ref[cut(a), cut(b)] = value
        for layer in range(2):
            weighted = rb_ref[layer, cut(a), :] * value
            for t in range(TILE // 8):
                sums[layer][b] = sums[layer][b] + weighted[t * 8 : (t + 1) * 8, :]

    for g in range(8):
        full = jnp.concatenate([o_ref[part % 2, 2 * g + part // 2] for part in range(4)], axis=0)
        if g in OFF:
            a, b = OFF[g]
            put(a, b, full)
            put(b, a, full.T)
        else:
            a, b = DIAG[g]
            turned = full.T
            diagonal = eo_ref[g // 7, 0:1, :]
            upper = jnp.where(row < col, full, jnp.where(row == col, diagonal, turned))
            put(a, a, upper)
            put(b, b, jnp.where(row < col, turned, full))
    for layer in range(2):
        for t in range(4):
            h_ref[layer, :, cut(t)] = sums[layer][t]


def exchange_kernel(
    slot_ref, hw_hbm, target_hbm, q_hbm, k_hbm,
    p_ref, s_ref, h_ref, rr_ref, w_ref, qk_ref, qt_ref, rb_ref,
    hw_ref, target_ref, sc_ref, x_ref, a_ref, y_ref, b_ref, z_ref, zn_ref, zf_ref,
    tn_ref, t_ref, to_ref, ta_ref, tb_ref, tt_ref, piece_ref, o_ref,
    e_ref, ey_ref, eb_ref, ez_ref, en_ref, ef_ref, ep_ref, eo_ref,
    sin, s0, r0, s1, r1, sz, rz, st, rt, s3, r3, s4, r4, es, er, relay,
):
    loads = [
        pltpu.make_async_copy(q_hbm.at[0], qk_ref.at[0, 0], sin.at[0]),
        pltpu.make_async_copy(k_hbm.at[0], qk_ref.at[0, 1], sin.at[0]),
        pltpu.make_async_copy(hw_hbm, hw_ref, sin.at[2]),
        pltpu.make_async_copy(q_hbm.at[1], qk_ref.at[1, 0], sin.at[1]),
        pltpu.make_async_copy(k_hbm.at[1], qk_ref.at[1, 1], sin.at[1]),
        pltpu.make_async_copy(target_hbm, target_ref, sin.at[3]),
    ]
    for c in loads:
        c.start()
    layer_pos = lax.axis_index("layer")
    head_pos = lax.axis_index("head")
    x = layer_pos % 4
    y_lo = layer_pos // 4
    core = head_pos % 2
    z = (head_pos // 2) % 16
    y_hi = head_pos // 32
    y = y_hi * 2 + y_lo
    group = y_hi * 4 + x
    other = 1 - core
    mine = group * 2 + y_lo
    sign = 1 - 2 * core

    def device(dx=0, dy=0, dz=0, flip=False):
        nx = (x + sign * dx + 4) % 4
        ny = (y + sign * dy + 4) % 4
        nz = (z + sign * dz + 16) % 16
        nc = other if flip else core
        return {"layer": (ny % 2) * 4 + nx, "head": (ny // 2) * 32 + nz * 2 + nc}

    def place(dx, dy):
        nx = (x + sign * dx + 4) % 4
        ny = (y + sign * dy + 4) % 4
        return ((ny // 2) * 4 + nx) * 2 + ny % 2

    def in_group(g, c):
        low = (y_lo + g // 4 + y_hi) % 2
        return {"layer": low * 4 + g % 4, "head": (g // 4) * 32 + z * 2 + c}

    def chip(p):
        return {"layer": (p % 2) * 4 + (p // 2) % 4, "head": (p // 8) * 32 + z * 2 + core}

    partner = device(flip=True)
    sent_to = pick(group, MIRROR)
    got_from = pick(group, MIRRORED)

    barrier = pltpu.get_barrier_semaphore()
    greeted = [device(dx, dy) for dx, dy in OFFSETS]
    greeted += [device(dz=d) for d in (3, -3, 2, -2, 1, -1)]
    greeted += [partner, in_group(sent_to, other), in_group(got_from, other)]
    for d in greeted:
        pl.semaphore_signal(barrier, inc=1, device_id=d, device_id_type=MESH)

    def ready(layer):
        pltpu.make_async_copy(qk_ref.at[layer], qk_ref.at[layer], sin.at[layer]).wait()
        if layer == 0:
            loads[2].wait()
            w = slot_weights(slot_ref, hw_ref)
            w_ref[...] = jnp.broadcast_to(w, (2, TILE))

    forward(w_ref, qk_ref, ready, sc_ref, p_ref, rb_ref, rr_ref, x_ref, e_ref)
    loads[5].wait()
    pl.semaphore_wait(barrier, len(greeted))

    def copy(src, dst, ssem, rsem, dev):
        return pltpu.make_async_remote_copy(
            src_ref=src, dst_ref=dst, send_sem=ssem, recv_sem=rsem, device_id=dev, device_id_type=MESH
        )

    def arrived(ref, rsem):
        copy(ref, ref, s0, rsem, partner).wait_recv()

    def left(ref, ssem):
        copy(ref, ref, ssem, r1, partner).wait_send()

    tile = target_ref.at[:, pl.ds(pl.multiple_of(x * TILE, TILE), TILE)]
    for d, slot in ((1, 1), (-1, 3), (2, 0), (-2, 4)):
        copy(tile, tn_ref.at[slot], st.at[0], rt.at[0], device(dz=d)).start()
    copy(tile, tn_ref.at[5], st.at[0], rt.at[4], device(dz=-3)).start()
    tn_ref[2] = target_ref[:, pl.ds(pl.multiple_of(x * TILE, TILE), TILE)]

    order = OFFSETS + [(0, 0)]
    copy(e_ref.at[other], a_ref.at[pl.ds(16 * ROWS, 8)], s0, r0.at[0], partner).start()
    for i, (dx, dy) in enumerate(order):
        copy(x_ref.at[other, place(-dx, -dy)], a_ref.at[pl.ds(i * ROWS, ROWS)], s0, r0.at[1 + i // 4], partner).start()

    arrived(a_ref.at[pl.ds(16 * ROWS, 8)], r0.at[0])
    ey_ref[...] = e_ref[core] + a_ref[16 * ROWS : 16 * ROWS + 8, :]
    owner = mine == core * 14
    owner_of_diagonal = {"layer": core * 3, "head": core * 33 + z * 2}

    @pl.when(jnp.logical_not(owner))
    def _():
        copy(ey_ref, eb_ref.at[mine], es.at[0], er.at[0], owner_of_diagonal).start()

    for i, (dx, dy) in enumerate(order):
        if i % 4 == 0:
            arrived(a_ref.at[pl.ds(i * ROWS, 4 * ROWS)], r0.at[1 + i // 4])
        summed = x_ref[core, place(dx, dy)] + a_ref[i * ROWS : (i + 1) * ROWS, :]
        if i < 15:
            y_ref[i] = summed
            copy(y_ref.at[i], b_ref.at[i], s1, r1, device(dx, dy)).start()
        else:
            total = summed

    arrived(t_ref.at[pl.ds(0, 4)], rt.at[0])
    pl.semaphore_signal(relay, inc=1, device_id=device(dz=-5), device_id_type=MESH)
    copy(tn_ref.at[pl.ds(0, 5)], t_ref.at[pl.ds(0, 5)], st.at[0], rt.at[1], device(dz=5)).start()
    arrived(tn_ref.at[5], rt.at[4])
    copy(tn_ref, t_ref.at[pl.ds(10, 6)], st.at[0], rt.at[1], device(dz=-5)).start()

    arrived(b_ref, r1)
    for i in range(15):
        total = total + b_ref[i]
    z_ref[0] = total
    near = (1, -1, 2, -2)
    for i, d in enumerate(near):
        copy(z_ref.at[0], zn_ref.at[i], sz.at[0], rz.at[0], device(dz=d)).start()
    @pl.when(owner)
    def _():
        eb_ref[mine] = ey_ref[...]
        arrived(eb_ref.at[pl.ds(0, 15)], er.at[0])
        acc = eb_ref[0]
        for i in range(1, 16):
            acc = acc + eb_ref[i]
        ez_ref[0] = acc
        for i, d in enumerate(near):
            copy(ez_ref.at[0], en_ref.at[i], es.at[1], er.at[1], device(dz=d)).start()

    pl.semaphore_wait(relay, 1)
    copy(z_ref.at[0], zn_ref.at[4], sz.at[0], rz.at[2], device(dz=8)).start()

    @pl.when(owner)
    def _():
        copy(ez_ref.at[0], en_ref.at[4], es.at[1], er.at[3], device(dz=8)).start()

    arrived(zn_ref.at[pl.ds(0, 4)], rz.at[0])
    for i in range(4):
        total = total + zn_ref[i]
    z_ref[1] = total
    for i, d in enumerate((5, -5)):
        copy(z_ref.at[1], zf_ref.at[i], sz.at[1], rz.at[1], device(dz=d)).start()

    @pl.when(owner)
    def _():
        arrived(en_ref.at[pl.ds(0, 4)], er.at[1])
        acc = ez_ref[0]
        for i in range(4):
            acc = acc + en_ref[i]
        ez_ref[1] = acc
        for i, d in enumerate((5, -5)):
            copy(ez_ref.at[1], ef_ref.at[i], es.at[2], er.at[2], device(dz=d)).start()

    arrived(t_ref.at[pl.ds(0, 11)], rt.at[1])
    for slot in range(16):
        to_ref[(z + sign * (slot - 7) + 16) % 16] = tn_ref[slot - 5] if 5 <= slot < 10 else t_ref[slot]
    keep = pick(group, KEEP)
    kept = to_ref.at[pl.ds(keep * 8, 8)]
    given = to_ref.at[pl.ds((1 - keep) * 8, 8)]
    copy(kept, ta_ref.at[core], st.at[1], rt.at[2], partner).start()
    copy(given, tb_ref.at[core], st.at[2], rt.at[3], in_group(sent_to, core)).start()
    copy(given, tb_ref.at[core], st.at[2], rt.at[3], in_group(sent_to, other)).start()
    ta_ref[core] = to_ref[pl.ds(keep * 8, 8)]
    for layer in range(2):
        qt_ref[layer] = qk_ref[layer, 0].astype(F32).T.astype(BF16)

    arrived(ta_ref.at[other], rt.at[2])
    arrived(tb_ref, rt.at[3])

    def joined(ref):
        return jnp.concatenate([ref[t % 2, t // 2] for t in range(16)], axis=0).astype(F32)

    row = lax.broadcasted_iota(jnp.int32, (TILE, TILE), 0)
    col = lax.broadcasted_iota(jnp.int32, (TILE, TILE), 1)
    first, second = joined(ta_ref), joined(tb_ref)
    first_t, second_t = first.T, second.T
    folded = jnp.where(row < col, first + first_t, second + second_t)
    on_diagonal = jnp.broadcast_to(group % 7, (TILE, TILE)) == 0
    tt_ref[...] = jnp.where(on_diagonal, folded, first + second_t)
    own = jnp.sum(jnp.where(row == col, first, 0.0), axis=0, keepdims=True)
    targets = tt_ref[pl.ds(pl.multiple_of((y_lo * 2 + core) * ROWS, ROWS), ROWS), :]

    arrived(zf_ref, rz.at[1])
    arrived(zn_ref.at[4], rz.at[2])
    total = total + zf_ref[0] + zf_ref[1] + zn_ref[4]
    piece_ref[...] = 2.0 * jax.nn.sigmoid(total) - targets
    for p in range(16):

        @pl.when(mine != p)
        def _(p=p):
            copy(piece_ref, o_ref.at[core, mine], s3, r3.at[mine // 4], chip(p)).start()

    keep_own = pltpu.make_async_copy(piece_ref, o_ref.at[core, mine], r3.at[mine // 4])
    keep_own.start()

    @pl.when(owner)
    def _():
        arrived(ef_ref, er.at[2])
        arrived(en_ref.at[4], er.at[3])
        acc = ez_ref[1] + ef_ref[0] + ef_ref[1] + en_ref[4]
        ep_ref[...] = 2.0 * jax.nn.sigmoid(acc) - 2.0 * own
        for dx, dy in OFFSETS:
            copy(ep_ref, eo_ref.at[core], es.at[3], er.at[4], device(dx, dy)).start()
        copy(ep_ref, eo_ref.at[core], es.at[4], er.at[5], partner).start()
        eo_ref[core] = ep_ref[...]

    for g in range(4):
        pieces = o_ref.at[core, pl.ds(4 * g, 4)]
        arrived(pieces, r3.at[g])
        copy(pieces, pieces, s4, r4, partner).start()

    @pl.when(jnp.logical_not(owner))
    def _():
        arrived(eo_ref.at[core], er.at[4])
        copy(eo_ref.at[core], eo_ref.at[core], es.at[4], er.at[5], partner).start()

    arrived(o_ref.at[other], r4)
    arrived(eo_ref.at[other], er.at[5])
    unpack(o_ref, eo_ref, rb_ref, s_ref, h_ref)

    left(a_ref, s0)
    left(b_ref, s1)
    left(zn_ref, sz.at[0])
    left(zf_ref, sz.at[1])
    left(t_ref, st.at[0])
    left(ta_ref.at[core], st.at[1])
    left(tb_ref, st.at[2])
    left(b_ref, s3)
    left(o_ref.at[core], s4)
    left(ep_ref, es.at[4])

    @pl.when(owner)
    def _():
        left(en_ref, es.at[1])
        left(ef_ref, es.at[2])
        left(eb_ref.at[pl.ds(0, 15)], es.at[3])

    @pl.when(jnp.logical_not(owner))
    def _():
        left(ey_ref, es.at[0])


def back_kernel(w_ref, qt_ref, qk_ref, p_ref, s_ref, h_ref, rr_ref, qg_hbm, kg_hbm, wg_hbm, d_ref, ds_ref, qg_ref, kg_ref, wg_ref, sems):
    scale = DH ** (-0.5)
    chunk = 32
    zero = jnp.zeros((8, L), F32)

    grads = []
    stores = []
    h_rows = []
    for layer in range(2):
        h_row = jnp.sum(h_ref[layer], axis=0, keepdims=True)
        quad = jnp.sum(h_row * rr_ref[layer : layer + 1, :], axis=1, keepdims=True)
        h_scaled = h_row * (1.0 / TOTAL)
        d_row = quad * (1.0 / (TOTAL * TOTAL)) - h_scaled
        for t in range(4):
            wide = jnp.broadcast_to(d_row[:, t * TILE : (t + 1) * TILE], (TILE, TILE))
            d_ref[layer, t * TILE : (t + 1) * TILE, :] = wide.T
        h_rows.append(h_scaled)
        grads.append(-quad * (0.5 / TOTAL))

    def map_rows(layer, i, acc):
        rows = slice(i * chunk, (i + 1) * chunk)
        s = s_ref[rows, :]
        probs = p_ref[layer, rows, :]
        wide = jnp.concatenate([d_ref[layer, rows, :]] * 4, axis=1)
        dprobs = s + wide - h_rows[layer]
        prod = probs * s
        for t in range(chunk // 8):
            acc = acc + prod[t * 8 : (t + 1) * 8, :]
        inner = jnp.sum(probs * dprobs, axis=1, keepdims=True)
        ds_ref[layer, rows, :] = (probs * (dprobs - inner)).astype(BF16)
        return acc

    def query_rows(layer, i, count):
        rows = slice(i * count, (i + 1) * count)
        qg = jnp.dot(ds_ref[layer, rows, :], qk_ref[layer, 1], preferred_element_type=F32)
        qg_ref[layer, rows, :] = (qg * (w_ref[layer : layer + 1, :] * scale)).astype(BF16)

    def key_rows(layer, i, count):
        rows = slice(i * count, (i + 1) * count)
        kg = jnp.dot(qt_ref[layer], ds_ref[layer, :, rows], preferred_element_type=F32)
        kg_ref[layer, rows, :] = (kg.T * (w_ref[layer : layer + 1, :] * scale)).astype(BF16)

    def store(src, dst, index):
        stores.append(pltpu.make_async_copy(src, dst, sems.at[index]))
        stores[-1].start()

    acc = zero
    for i in range(16):
        acc = map_rows(0, i, acc)
        if i == 9:
            query_rows(0, 0, 256)
    grads[0] = grads[0] + jnp.sum(jnp.sum(acc, axis=0, keepdims=True), axis=1, keepdims=True)
    acc = zero
    for i in range(16):
        acc = map_rows(1, i, acc)
        if i == 1:
            query_rows(0, 1, 256)
        if i == 3 or i == 7:
            key_rows(0, i // 4, 256)
        if i == 9:
            query_rows(1, 0, 256)
            store(qg_ref.at[1, pl.ds(0, 256)], qg_hbm.at[1, pl.ds(0, 256)], 3)
    grads[1] = grads[1] + jnp.sum(jnp.sum(acc, axis=0, keepdims=True), axis=1, keepdims=True)
    lane = lax.broadcasted_iota(jnp.int32, (1, 2), 1)
    wg_ref[...] = jnp.where(lane == 0, grads[0], grads[1])
    store(wg_ref, wg_hbm, 5)
    store(qg_ref.at[0], qg_hbm.at[0], 0)
    store(kg_ref.at[0], kg_hbm.at[0], 1)
    for i in range(2):
        key_rows(1, i, 256)
    store(kg_ref.at[1], kg_hbm.at[1], 2)
    query_rows(1, 1, 256)
    store(qg_ref.at[1, pl.ds(256, 256)], qg_hbm.at[1, pl.ds(256, 256)], 4)
    for c in stores:
        c.wait()


def vmem():
    return pl.BlockSpec(memory_space=pltpu.VMEM)


def smem():
    return pl.BlockSpec(memory_space=pltpu.SMEM)


def hbm():
    return pl.BlockSpec(memory_space=pltpu.HBM)


def on_device(queries, keys, head_weight, slot_head, target):
    q = queries.reshape(2, L, DH)
    k = keys.reshape(2, L, DH)
    dma = pltpu.SemaphoreType.DMA
    probs, s_map, h, rr, w, qk, q_turned = pl.pallas_call(
        exchange_kernel,
        out_shape=(
            pltpu.VMEM((2, L, L), F32),
            pltpu.VMEM((L, L), F32),
            pltpu.VMEM((2, 8, L), F32),
            pltpu.VMEM((2, L), F32),
            pltpu.VMEM((2, TILE), F32),
            pltpu.VMEM((2, 2, L, DH), BF16),
            pltpu.VMEM((2, DH, L), BF16),
        ),
        in_specs=[smem()] + [hbm()] * 4,
        out_specs=(vmem(),) * 7,
        scratch_shapes=[
            pltpu.VMEM((2, L, TILE), F32),
            pltpu.VMEM((2, 40), F32),
            pltpu.VMEM((8, L), jnp.int32),
            pltpu.VMEM((2, L, L), F32),
            pltpu.VMEM((2, 16, ROWS, TILE), F32),
            pltpu.VMEM((16 * ROWS + 8, TILE), F32),
            pltpu.VMEM((15, ROWS, TILE), F32),
            pltpu.VMEM((15, ROWS, TILE), F32),
            pltpu.VMEM((3, ROWS, TILE), F32),
            pltpu.VMEM((5, ROWS, TILE), F32),
            pltpu.VMEM((2, ROWS, TILE), F32),
            pltpu.VMEM((6, 8, TILE), jnp.int32),
            pltpu.VMEM((16, 8, TILE), jnp.int32),
            pltpu.VMEM((16, 8, TILE), jnp.int32),
            pltpu.VMEM((2, 8, 8, TILE), jnp.int32),
            pltpu.VMEM((2, 8, 8, TILE), jnp.int32),
            pltpu.VMEM((TILE, TILE), F32),
            pltpu.VMEM((ROWS, TILE), F32),
            pltpu.VMEM((2, 16, ROWS, TILE), F32),
            pltpu.VMEM((2, 8, TILE), F32),
            pltpu.VMEM((8, TILE), F32),
            pltpu.VMEM((16, 8, TILE), F32),
            pltpu.VMEM((3, 8, TILE), F32),
            pltpu.VMEM((5, 8, TILE), F32),
            pltpu.VMEM((2, 8, TILE), F32),
            pltpu.VMEM((8, TILE), F32),
            pltpu.VMEM((2, 8, TILE), F32),
            dma((4,)), dma, dma((5,)), dma, dma, dma((2,)), dma((3,)), dma((3,)), dma((5,)),
            dma, dma((4,)), dma, dma, dma((5,)), dma((6,)), pltpu.SemaphoreType.REGULAR,
        ],
        compiler_params=pltpu.CompilerParams(collective_id=0, has_side_effects=True, vmem_limit_bytes=16 << 20),
    )(slot_head, *[pltpu.with_memory_space_constraint(v, pltpu.HBM) for v in (head_weight, target, q, k)])
    qg, kg, wg = pl.pallas_call(
        back_kernel,
        out_shape=(
            jax.ShapeDtypeStruct((2, L, DH), BF16),
            jax.ShapeDtypeStruct((2, L, DH), BF16),
            jax.ShapeDtypeStruct((1, 2), F32),
        ),
        in_specs=[vmem()] * 7,
        out_specs=(hbm(), hbm(), hbm()),
        scratch_shapes=[
            pltpu.VMEM((2, L, TILE), F32),
            pltpu.VMEM((2, L, L), BF16),
            pltpu.VMEM((2, L, DH), BF16),
            pltpu.VMEM((2, L, DH), BF16),
            pltpu.VMEM((1, 2), F32),
            pltpu.SemaphoreType.DMA((6,)),
        ],
        compiler_params=pltpu.CompilerParams(vmem_limit_bytes=16 << 20),
    )(w, q_turned, qk, probs, s_map, h, rr)
    return (qg.reshape(2, 1, L, DH), kg.reshape(2, 1, L, DH), wg.reshape(2, 1))


def solution(mesh):
    placed = (
        P("layer", "head", None, None),
        P("layer", "head", None, None),
        P("layer", None),
        P("head"),
        P("head", None),
    )
    return jax.shard_map(
        on_device,
        mesh=mesh,
        in_specs=placed,
        out_specs=(P("layer", "head", None, None), P("layer", "head", None, None), P("layer", "head")),
        check_vma=False,
    )
```
